128 devices in a mesh: seq: 32 (over y, z, core), head: 4 (over x).
Axes of the slice: x: 4, y: 4, z: 4, core: 2. Of those that a mesh axis runs over, the one named last changes fastest.
Arguments:
- queries: bfloat16 [32768, 1024], P('seq', 'head'), may hold values from -6 to 6
- key_rows: bfloat16 [32768, 1024], P('seq', 'head'), may hold values from -6 to 6
- value_rows: bfloat16 [32768, 1024], P('seq', 'head'), may hold values from -6 to 6
- attn_out: bfloat16 [32768, 1024], P('seq', 'head'), may hold values from -6 to 6
- gate_pre: bfloat16 [32768, 1024], P('seq', 'head'), may hold values from -6 to 6
- out_grad: bfloat16 [32768, 1024], P('seq', 'head'), may hold values from -6 to 6
- segments: int32 [32768], P('seq'), may hold values from 0 to 7, never falling along the last dimension, each value on 1 to 6145 neighbouring positions
- projections: bfloat16 [4, 1024, 1024], P(None, None, 'head'), may hold values from -0.1875 to 0.1875
Outputs:
- input_grad: bfloat16 [32768, 1024], P('seq', 'head')
The draws below stay inside these ranges and needn't reach their ends.
Inputs may be any that keep to these rules, and one draw needn't show every extreme that they name: `segments`: each user's rows are contiguous and ordered; a user has 1 to 6145 rows and one user has exactly 6145, so no user spans more than 6 + 1 = 7 shards of 1024 rows.
All inputs are finite; a program needn't handle non-finite values.
Results may differ from the reference program's by a relative error of at most 0.0064.
Values may be sent and summed in bfloat16 or wider, within the bound.
No kernel may reach another device: no remote copies, remote signals or barrier semaphores. Data moves between devices by JAX's collectives and lax.ppermute only.
A program may use at most 128 MiB of HBM per device.

```python
import math
import jax
import jax.numpy as jnp
import numpy as np
from jax import lax

D = 1024
HEAD_DIM = 128
WINDOW = 6
ROWS = 1024
TOKENS = 32768
USERS = 8
N_SEQ = 32


def shard_levels(rng, extent, pieces, low, high):
    loudness, own = 1.0, jax.random.fold_in(rng, 6)
    for axis_at, parts in pieces:
        draws = jnp.exp(jax.random.uniform(jax.random.fold_in(own, axis_at), (parts,), jnp.float32, low / len(pieces), high / len(pieces)))
        loudness = loudness * jnp.repeat(draws, extent[axis_at] // parts).reshape([-1 if axis == axis_at else 1 for axis in range(len(extent))])
    return loudness


def split_up(count, total, reach, skew):
    weights = [(1 << 20) // math.isqrt(grade ** skew) + 1 for grade in range(2, count + 1)]
    rest, given = total - reach - (count - 1), [1] * (count - 1)
    while rest > 0:
        candidates = [i for i in range(count - 1) if given[i] < reach]
        mass, left = sum([weights[i] for i in candidates]), rest
        for i in candidates:
            addition = min(reach - given[i], max(1, left * weights[i] // mass), rest)
            given[i] = given[i] + addition
            rest = rest - addition
    return np.array([reach] + given)


def uneven(key, count, total, bound, lean):
    if count == 2:
        one = jax.random.randint(key, (), max(1, total - bound), min(bound, total - 1) + 1)
        return jnp.stack([one, total - one])
    lengths = jnp.asarray(split_up(count, total, bound, lean), jnp.int32)
    couples = (count - 1) // 2
    donor, receiver = lengths[1:1 + 2 * couples:2], lengths[2:2 + 2 * couples:2]
    slack = jnp.minimum(donor - 1, bound - receiver)
    shifted = jax.random.randint(jax.random.fold_in(key, 1), (couples,), 0, 1 << 20) % (slack + 1)
    lengths = lengths.at[1:1 + 2 * couples:2].set(donor - shifted).at[2:2 + 2 * couples:2].set(receiver + shifted)
    return lengths[jax.random.permutation(jax.random.fold_in(key, 2), count)]


def noise(own_key, extent, spread, most, split=(), kind=jnp.bfloat16):
    drawn = jax.random.normal(own_key, extent, jnp.float32) * spread
    if len(split) > 0:
        drawn = shard_levels(own_key, extent, split, -0.22, 0.18) * drawn
    return jnp.clip(drawn, min=-most, max=most).astype(kind)


def setup_inputs(seed: int = 0) -> dict:
    seeds = jax.random.split(jax.random.key(seed), 9)
    return {
        "queries": noise(seeds[0], (TOKENS, D), 1.0, 6.0, ((0, 32), (1, 4))),
        "key_rows": noise(seeds[1], (TOKENS, D), 1.0, 6.0, ((0, 32), (1, 4))),
        "value_rows": noise(seeds[2], (TOKENS, D), 1.0, 6.0, ((0, 32), (1, 4))),
        "attn_out": noise(seeds[3], (TOKENS, D), 1.0, 6.0, ((0, 32), (1, 4))),
        "gate_pre": noise(seeds[4], (TOKENS, D), 1.0, 6.0, ((0, 32), (1, 4))),
        "out_grad": noise(seeds[5], (TOKENS, D), 1.0, 6.0, ((0, 32), (1, 4))),
        "segments": jnp.searchsorted(jnp.cumsum(uneven(seeds[6], USERS, TOKENS, 6 * ROWS + 1, 0)), jnp.arange(TOKENS), side="right").astype(jnp.int32),
        "projections": noise(seeds[7], (4, D, D), D ** -0.5, 0.1875, ((2, 4),)),
    }


def silu_slope(values_in):
    sigma = jax.nn.sigmoid(values_in)
    return sigma * (1.0 + values_in * (1.0 - sigma))

def rounded(values_in):
    return lax.optimization_barrier(values_in.astype(jnp.bfloat16)).astype(jnp.float32)

def norm_backward(attn_out, gate_pre, out_grad):
    row_count, width = attn_out.shape
    head_count = width // HEAD_DIM
    saved = attn_out.astype(jnp.float32).reshape(row_count, head_count, HEAD_DIM)
    centred = saved - lax.optimization_barrier(jnp.mean(saved, axis=-1, keepdims=True))
    inverse = lax.rsqrt(lax.optimization_barrier(jnp.mean(centred * centred, axis=-1, keepdims=True)) + 1e-06)
    normed = centred * inverse
    gate_in = gate_pre.astype(jnp.float32)
    grad_in = out_grad.astype(jnp.float32)
    gate_grad = grad_in * normed.reshape(row_count, width) * silu_slope(gate_in)
    normed_grad = (grad_in * jax.nn.silu(gate_in)).reshape(row_count, head_count, HEAD_DIM)
    attn_grad = inverse * (normed_grad - lax.optimization_barrier(jnp.mean(normed_grad, axis=-1, keepdims=True)) - normed * lax.optimization_barrier(jnp.mean(normed_grad * normed, axis=-1, keepdims=True)))
    return (attn_grad.reshape(row_count, width).astype(jnp.bfloat16), gate_grad.astype(jnp.bfloat16))

def reference(queries, key_rows, value_rows, attn_out, gate_pre, out_grad, segments, projections):
    attn_grad, gate_grad = norm_backward(attn_out, gate_pre, out_grad)
    head_count = D // HEAD_DIM
    scale = HEAD_DIM ** (-0.5)
    causal = jnp.arange(ROWS)[:, None] >= jnp.arange(ROWS)[None, :]

    def take(source, start):
        return lax.dynamic_slice_in_dim(source, start, ROWS, 0)

    def split_heads(source):
        return source.astype(jnp.float32).reshape(ROWS, head_count, HEAD_DIM)

    def per_shard(carry, shard):
        key_acc, value_acc = carry
        start = (shard * ROWS).astype(jnp.int32)
        query_blk = split_heads(take(queries, start))
        grad_blk = split_heads(take(attn_grad, start))
        owner_q = take(segments, start)
        query_acc = jnp.zeros((ROWS, head_count, HEAD_DIM), jnp.float32)
        for distance in range(WINDOW + 1):
            source_shard = jnp.maximum(shard - distance, 0).astype(jnp.int32)
            key_start = (source_shard * ROWS).astype(jnp.int32)
            key_blk = split_heads(take(key_rows, key_start))
            value_blk = split_heads(take(value_rows, key_start))
            owner_k = take(segments, key_start)
            allowed = (owner_q[:, None] == owner_k[None, :]) & (shard - distance >= 0)
            if distance == 0:
                allowed = allowed & causal
            scores = jnp.einsum('qhd,khd->hqk', query_blk, key_blk) * scale
            weights = rounded(jnp.where(allowed, jax.nn.silu(scores), 0.0))
            slope_in = jnp.einsum('qhd,khd->hqk', grad_blk, value_blk)
            score_grad = rounded(jnp.where(allowed, slope_in * silu_slope(scores) * scale, 0.0))
            query_acc = query_acc + jnp.einsum('hqk,khd->qhd', score_grad, key_blk)
            key_add = jnp.einsum('hqk,qhd->khd', score_grad, query_blk).reshape(ROWS, D)
            value_add = jnp.einsum('hqk,qhd->khd', weights, grad_blk).reshape(ROWS, D)
            key_acc = lax.dynamic_update_slice_in_dim(key_acc, take(key_acc, key_start) + key_add, key_start, 0)
            value_acc = lax.dynamic_update_slice_in_dim(value_acc, take(value_acc, key_start) + value_add, key_start, 0)
        return ((key_acc, value_acc), query_acc.reshape(ROWS, D))
    zero_grads = jnp.zeros((TOKENS, D), jnp.float32)
    (key_acc, value_acc), query_parts = lax.scan(per_shard, (zero_grads, zero_grads), jnp.arange(N_SEQ, dtype=jnp.int32))
    query_acc = query_parts.reshape(TOKENS, D)
    stacked = jnp.stack([query_acc.astype(jnp.bfloat16), key_acc.astype(jnp.bfloat16), value_acc.astype(jnp.bfloat16), gate_grad])
    result = jnp.einsum('prh,pdh->rd', stacked.astype(jnp.float32), projections.astype(jnp.float32))
    return result.astype(jnp.bfloat16)
```

```python
import jax
import jax.numpy as jnp
from jax import lax
from jax.experimental import pallas as pl
from jax.experimental.pallas import tpu as pltpu
from jax.sharding import PartitionSpec as P

HEAD_DIM = 128
ROWS = 1024
PAIR = 2 * ROWS
SEG_ROWS = 16
TILE = 512
TILES = PAIR // TILE
HALF_SCALE = 0.5 * HEAD_DIM ** (-0.5)
VMEM = pl.BlockSpec(memory_space=pltpu.VMEM)
SMEM = pl.BlockSpec(memory_space=pltpu.SMEM)
BF16, F32 = jnp.bfloat16, jnp.float32


def cost(flops, transcendentals, size):
    return pl.CostEstimate(flops=flops, transcendentals=transcendentals, bytes_accessed=size)


def params():
    return pltpu.CompilerParams(vmem_limit_bytes=28 * 2**20)


def shift(block, distance):
    devices = range(lax.axis_size("seq"))
    return lax.ppermute(block, "seq", [(i, i + distance) for i in devices if i + distance in devices])


def swap(block):
    return lax.ppermute(block, "seq", [(i, i ^ 1) for i in range(lax.axis_size("seq"))])


def silu_slope(v):
    sigma = jax.nn.sigmoid(v)
    return sigma * (1.0 + v * (1.0 - sigma))


def prepare_kernel(core, q, k, v, o, gate, grad, keep, send, gate_grad):
    for slot, out in ((0, keep), (1, send)):
        head = core[0] if slot == 0 else 1 - core[0]
        cols = pl.ds(pl.multiple_of(head * HEAD_DIM, HEAD_DIM), HEAD_DIM)
        saved = o[:, cols].astype(F32)
        centred = saved - jnp.mean(saved, axis=-1, keepdims=True)
        inverse = lax.rsqrt(jnp.mean(centred * centred, axis=-1, keepdims=True) + 1e-06)
        normed = centred * inverse
        gate_in = gate[:, cols].astype(F32)
        grad_in = grad[:, cols].astype(F32)
        gate_grad[:, cols] = (grad_in * normed * silu_slope(gate_in)).astype(BF16)
        g = grad_in * jax.nn.silu(gate_in)
        attn_grad = inverse * (
            g
            - jnp.mean(g, axis=-1, keepdims=True)
            - normed * jnp.mean(g * normed, axis=-1, keepdims=True)
        )
        out[:, 0:128] = q[:, cols]
        out[:, 128:256] = attn_grad.astype(BF16)
        out[:, 256:384] = k[:, cols]
        out[:, 384:512] = v[:, cols]


def prepare(core, *arrays):
    rows = 256
    wide = pl.BlockSpec((rows, 2 * HEAD_DIM), lambda i, c: (i, 0))
    packed = pl.BlockSpec((rows, 4 * HEAD_DIM), lambda i, c: (i, 0))
    return pl.pallas_call(
        prepare_kernel,
        grid_spec=pltpu.PrefetchScalarGridSpec(
            num_scalar_prefetch=1,
            grid=(ROWS // rows,),
            in_specs=[wide] * 6,
            out_specs=[packed, packed, wide],
        ),
        out_shape=[
            jax.ShapeDtypeStruct((ROWS, 4 * HEAD_DIM), BF16),
            jax.ShapeDtypeStruct((ROWS, 4 * HEAD_DIM), BF16),
            jax.ShapeDtypeStruct((ROWS, 2 * HEAD_DIM), BF16),
        ],
        compiler_params=params(),
        cost_estimate=cost(30 * ROWS * 256, 2 * ROWS * 256, 11 * ROWS * 512),
        name="prepare",
    )(core, *arrays)


def pairs_kernel(diagonal, core, query, seg_k, kv_keep, kv_recv, dq_out, dkv_out,
                 kv, dq, dk, dv, row_q, col_k, bound):
    dq[...] = jnp.zeros_like(dq)
    dk[...] = jnp.zeros_like(dk)
    dv[...] = jnp.zeros_like(dv)
    kv[0:ROWS] = kv_keep[...]
    kv[ROWS:PAIR] = kv_recv[...]
    users_q = query[PAIR:PAIR + SEG_ROWS].astype(F32)
    users_k = seg_k[...].astype(F32)
    for r in range(PAIR // 256):
        row_q[:, r * 256:(r + 1) * 256] = users_q[r:r + 1]
        for half in range(2):
            start = r * 256 + half * 128
            one = users_k[r:r + 1, half * 128:half * 128 + 128]
            col_k[start:start + 128] = jnp.transpose(jnp.broadcast_to(one, (128, 128)))
    for b in range(TILES):
        rows = slice(b * TILE // 256, (b + 1) * TILE // 256)
        bound[0, b] = jnp.min(users_q[rows])
        bound[1, b] = jnp.max(users_q[rows])
        bound[2, b] = jnp.min(users_k[rows])
        bound[3, b] = jnp.max(users_k[rows])
    offset = core[0] * ROWS
    last = (((1,), (1,)), ((), ()))
    first = (((0,), (0,)), ((), ()))

    def tile(kt, qt, masked):
        ks = pl.ds(pl.multiple_of(kt * TILE, TILE), TILE)
        qs = pl.ds(pl.multiple_of(qt * TILE, TILE), TILE)
        key, value = kv[ks, 0:128], kv[ks, 128:256]
        q, g = query[qs, 0:128], query[qs, 128:256]
        s = lax.dot_general(key, q, last, preferred_element_type=F32)
        p = lax.dot_general(value, g, last, preferred_element_type=F32)
        y = s * HALF_SCALE
        if masked:
            allowed = col_k[ks, 0:1] == row_q[:, qs]
            if diagonal:
                ahead = (qt * TILE + offset) % PAIR - (kt * TILE + offset) % PAIR
                allowed = allowed & (
                    lax.broadcasted_iota(jnp.int32, (TILE, TILE), 1) + ahead
                    >= lax.broadcasted_iota(jnp.int32, (TILE, TILE), 0)
                )
            y = jnp.where(allowed, y, -64.0)
        t = jnp.tanh(y)
        u = 1.0 + t
        w = y * u
        ds = (p * (u + w * (1.0 - t))).astype(BF16)
        w = w.astype(BF16)
        dv[ks, :] += jnp.dot(w, g, preferred_element_type=F32)
        dk[ks, :] += jnp.dot(ds, q, preferred_element_type=F32)
        dq[qs, :] += lax.dot_general(ds, key, first, preferred_element_type=F32)

    def over_keys(kt, carry):
        def over_queries(qt, carry):
            q_lo, q_hi, k_lo, k_hi = bound[0, qt], bound[1, qt], bound[2, kt], bound[3, kt]
            some = (q_lo <= k_hi) & (q_hi >= k_lo)
            every = (q_lo == k_hi) & (q_hi == k_lo)
            if diagonal:
                q_at = (qt * TILE + offset) % PAIR
                k_at = (kt * TILE + offset) % PAIR
                some = some & (q_at >= k_at)
                every = every & (q_at > k_at)
            pl.when(some & jnp.logical_not(every))(lambda: tile(kt, qt, True))
            pl.when(every)(lambda: tile(kt, qt, False))
            return carry

        return lax.fori_loop(0, TILES, over_queries, carry)

    lax.fori_loop(0, TILES, over_keys, 0)
    dq_out[...] = (dq[...] * HALF_SCALE).astype(BF16)
    dkv_out[:, 0:128] = (dk[...] * HALF_SCALE).astype(BF16)
    dkv_out[:, 128:256] = dv[...].astype(BF16)


def pairs(core, query, seg_k, keep, recv, diagonal):
    kv_spec = pl.BlockSpec((ROWS, 256), lambda i: (0, 1))
    whole = lambda rows, cols: pl.BlockSpec((rows, cols), lambda i: (0, 0))
    area = PAIR * PAIR // (2 if diagonal else 1)
    return pl.pallas_call(
        lambda *refs: pairs_kernel(diagonal, *refs),
        grid=(1,),
        in_specs=[SMEM, whole(PAIR + SEG_ROWS, 256), whole(SEG_ROWS, 256), kv_spec, kv_spec],
        out_specs=[whole(PAIR, 128), whole(PAIR, 256)],
        out_shape=[
            jax.ShapeDtypeStruct((PAIR, 128), BF16),
            jax.ShapeDtypeStruct((PAIR, 256), BF16),
        ],
        scratch_shapes=[
            pltpu.VMEM((PAIR, 256), BF16),
            pltpu.VMEM((PAIR, 128), F32),
            pltpu.VMEM((PAIR, 128), F32),
            pltpu.VMEM((PAIR, 128), F32),
            pltpu.VMEM((1, PAIR), F32),
            pltpu.VMEM((PAIR, 128), F32),
            pltpu.SMEM((4, TILES), F32),
        ],
        compiler_params=params(),
        cost_estimate=cost(20 * area * 128, area, 8 * PAIR * 256),
        name="pairs_own" if diagonal else "pairs_far",
    )(core, query, seg_k, keep, recv)


def project_kernel(place, mine, other, gate_grad, weights, out1, out2, out3, own):
    core, x = place[0], place[1]
    a = mine[...]
    b = other[...]
    first = core == 0
    blocks = []
    for p in range(3):
        cols = slice(p * 128, (p + 1) * 128)
        blocks.append(jnp.where(first, a[:, cols], b[:, cols]))
        blocks.append(jnp.where(first, b[:, cols], a[:, cols]))
    for step, out in ((1, out1), (2, out2), (3, out3), (4, own)):
        dest = lax.rem(x + step, 4)
        ds = pl.ds(pl.multiple_of(dest * 256, 256), 256)
        acc = lax.dot_general(gate_grad[...], weights[3, ds, :], (((1,), (1,)), ((), ())),
                              preferred_element_type=F32)
        for p in range(3):
            left = jnp.concatenate([blocks[2 * p], blocks[2 * p + 1]], axis=1)
            acc += lax.dot_general(left, weights[p, ds, :], (((1,), (1,)), ((), ())),
                                   preferred_element_type=F32)
        out[...] = acc.astype(out.dtype)


def project(place, mine, other, gate_grad, weights):
    part = jax.ShapeDtypeStruct((ROWS, 256), BF16)
    return pl.pallas_call(
        project_kernel,
        in_specs=[SMEM, VMEM, VMEM, VMEM, VMEM],
        out_specs=[VMEM] * 4,
        out_shape=[part, part, part, jax.ShapeDtypeStruct((ROWS, 256), F32)],
        compiler_params=params(),
        cost_estimate=cost(2 * ROWS * 1024 * 1024, 0, 8 * ROWS * 1024),
        name="project",
    )(place, mine, other, gate_grad, weights)


def per_device(queries, key_rows, value_rows, attn_out, gate_pre, out_grad, segments, projections):
    core = lax.axis_index("seq") % 2
    head = lax.axis_index("head")
    core_at = core.reshape(1).astype(jnp.int32)
    keep, send, gate_grad = prepare(
        core_at, queries, key_rows, value_rows, attn_out, gate_pre, out_grad
    )
    users = (segments + 1).astype(BF16)
    recv = swap(send)
    users_pair = jnp.concatenate([users, swap(users)])
    seg = jnp.pad(users_pair.reshape(PAIR // 256, 256), ((0, SEG_ROWS - PAIR // 256), (0, 0)))
    query = jnp.concatenate([keep[:, :256], recv[:, :256], seg])
    from1 = shift(query, -2)
    from3 = shift(query, -6)
    from2 = shift(from1, -2)
    dq0, dkv0 = pairs(core_at, query, seg, keep, recv, True)
    dq1, dkv1 = pairs(core_at, from1, seg, keep, recv, False)
    from3, dq1 = lax.optimization_barrier((from3, dq1))
    dq3, dkv3 = pairs(core_at, from3, seg, keep, recv, False)
    from2, dq3 = lax.optimization_barrier((from2, dq3))
    dq2, dkv2 = pairs(core_at, from2, seg, keep, recv, False)
    back1, back3, back2 = shift(dq1, 2), shift(dq3, 6), shift(dq2, 4)
    add = lambda *terms: sum(t.astype(F32) for t in terms).astype(BF16)
    dq = add(dq0, back1, back3, back2)
    dkv = add(dkv0, dkv1, dkv3, dkv2)
    grads = jnp.concatenate([dq, dkv], axis=1)
    mine, other = grads[:ROWS], swap(grads[ROWS:])
    place = jnp.stack([core, head]).astype(jnp.int32)
    part1, part2, part3, own = project(place, mine, other, gate_grad, projections)
    turn = lambda block, by: lax.ppermute(block, "head", [(i, (i + by) % 4) for i in range(4)])
    total = own + turn(part1, 1).astype(F32) + turn(part2, 2).astype(F32) + turn(part3, 3).astype(F32)
    return total.astype(BF16)


def solution(mesh):
    return jax.shard_map(
        per_device,
        mesh=mesh,
        in_specs=(
            P("seq", "head"),
            P("seq", "head"),
            P("seq", "head"),
            P("seq", "head"),
            P("seq", "head"),
            P("seq", "head"),
            P("seq"),
            P(None, None, "head"),
        ),
        out_specs=P("seq", "head"),
        check_vma=False,
    )
```

```python
import jax
import jax.numpy as jnp
from jax import lax
from jax.experimental import pallas as pl
from jax.experimental.pallas import tpu as pltpu
from jax.sharding import PartitionSpec as P

HEAD_DIM = 128
ROWS = 1024
PAIR = 2 * ROWS
SEG_ROWS = 16
TILE = 512
TILES = PAIR // TILE
HALF_SCALE = 0.5 * HEAD_DIM ** (-0.5)
VMEM = pl.BlockSpec(memory_space=pltpu.VMEM)
SMEM = pl.BlockSpec(memory_space=pltpu.SMEM)
BF16, F32 = jnp.bfloat16, jnp.float32


def cost(flops, transcendentals, size):
    return pl.CostEstimate(flops=flops, transcendentals=transcendentals, bytes_accessed=size)


def params(mib):
    return pltpu.CompilerParams(vmem_limit_bytes=mib * 2**20)


def shift(block, distance):
    devices = range(lax.axis_size("seq"))
    return lax.ppermute(block, "seq", [(i, i + distance) for i in devices if i + distance in devices])


def swap(block):
    return lax.ppermute(block, "seq", [(i, i ^ 1) for i in range(lax.axis_size("seq"))])


def silu_slope(v):
    sigma = jax.nn.sigmoid(v)
    return sigma * (1.0 + v * (1.0 - sigma))


def prepare_kernel(core, q, k, v, o, gate, grad, keep, send, gate_grad):
    for slot, out in ((0, keep), (1, send)):
        head = core[0] if slot == 0 else 1 - core[0]
        cols = pl.ds(pl.multiple_of(head * HEAD_DIM, HEAD_DIM), HEAD_DIM)
        saved = o[:, cols].astype(F32)
        centred = saved - jnp.mean(saved, axis=-1, keepdims=True)
        inverse = lax.rsqrt(jnp.mean(centred * centred, axis=-1, keepdims=True) + 1e-06)
        normed = centred * inverse
        gate_in = gate[:, cols].astype(F32)
        grad_in = grad[:, cols].astype(F32)
        gate_grad[:, cols] = (grad_in * normed * silu_slope(gate_in)).astype(BF16)
        g = grad_in * jax.nn.silu(gate_in)
        attn_grad = inverse * (
            g
            - jnp.mean(g, axis=-1, keepdims=True)
            - normed * jnp.mean(g * normed, axis=-1, keepdims=True)
        )
        out[:, 0:128] = q[:, cols]
        out[:, 128:256] = attn_grad.astype(BF16)
        out[:, 256:384] = k[:, cols]
        out[:, 384:512] = v[:, cols]


def prepare(core, *arrays):
    rows = 256
    wide = pl.BlockSpec((rows, 2 * HEAD_DIM), lambda i, c: (i, 0))
    packed = pl.BlockSpec((rows, 4 * HEAD_DIM), lambda i, c: (i, 0))
    return pl.pallas_call(
        prepare_kernel,
        grid_spec=pltpu.PrefetchScalarGridSpec(
            num_scalar_prefetch=1,
            grid=(ROWS // rows,),
            in_specs=[wide] * 6,
            out_specs=[packed, packed, wide],
        ),
        out_shape=[
            jax.ShapeDtypeStruct((ROWS, 4 * HEAD_DIM), BF16),
            jax.ShapeDtypeStruct((ROWS, 4 * HEAD_DIM), BF16),
            jax.ShapeDtypeStruct((ROWS, 2 * HEAD_DIM), BF16),
        ],
        compiler_params=params(60),
        cost_estimate=cost(30 * ROWS * 256, 2 * ROWS * 256, 11 * ROWS * 512),
        name="prepare",
    )(core, *arrays)


def pairs_kernel(kind, sources, *refs):
    own, near = kind == "own", kind == "near"
    q_in, k_in = refs[:sources], refs[sources:2 * sources]
    outs = refs[2 * sources:4 * sources]
    q, k, dq, dk, dv, row_q, col_k, bound, chip, todo, w0, d0, w1, d1, sem = refs[4 * sources:]
    wide = PAIR + SEG_ROWS
    copies = []
    for i in range(sources):
        at = pl.ds(i * wide, wide)
        copies.append(pltpu.make_async_copy(q_in[i], q.at[at], sem.at[2 * i]))
        copies.append(pltpu.make_async_copy(k_in[i], k.at[at], sem.at[2 * i + 1]))
    for copy in copies:
        copy.start()
    dq[...] = jnp.zeros_like(dq)
    dk[...] = jnp.zeros_like(dk)
    dv[...] = jnp.zeros_like(dv)
    for copy in copies:
        copy.wait()
    blocks = PAIR // 256
    for i in range(sources):
        at = slice(i * wide + PAIR, (i + 1) * wide)
        users_q, users_k = q[at].astype(F32), k[at].astype(F32)
        for r in range(blocks):
            start = i * PAIR + r * 256
            row_q[:, start:start + 256] = users_q[r:r + 1]
        padded = jnp.concatenate([users_k, jnp.zeros((128 - SEG_ROWS, 256), F32)])
        for half in range(2):
            turned = jnp.transpose(padded[:, half * 128:half * 128 + 128])
            for r in range(blocks):
                start = i * PAIR + r * 256 + half * 128
                col_k[start:start + 128] = jnp.broadcast_to(turned[:, r:r + 1], (128, 128))
        for b in range(TILES):
            rows = slice(b * TILE // 256, (b + 1) * TILE // 256)
            bound[0, i * TILES + b] = jnp.min(users_q[rows])
            bound[1, i * TILES + b] = jnp.max(users_q[rows])
            bound[2, i * TILES + b] = jnp.min(users_k[rows])
            bound[3, i * TILES + b] = jnp.max(users_k[rows])
        first_q, last_q = bound[0, i * TILES], bound[1, (i + 1) * TILES - 1]
        first_k, last_k = bound[2, i * TILES], bound[3, (i + 1) * TILES - 1]
        chip[i] = (first_q == last_q).astype(jnp.int32)
        chip[2 + i] = (first_k == last_k).astype(jnp.int32)
    row_q[:, sources * PAIR:] = jnp.full((1, TILE), -1.0, F32)

    count = jnp.int32(0)
    for qs in range(sources):
        for ks in range(sources):
            for kt in range(TILES):
                here = jnp.int32(1)
                if near and (qs, ks) != (1, 1):
                    late, early = chip[qs], chip[2 + ks]
                    if (qs, ks) == (1, 0):
                        here = jnp.where(early == 0, 1, late * (1 - kt % 2))
                    else:
                        here = early * jnp.where(late == 0, 1, kt % 2)
                for qt in range(TILES):
                    if (own and qt < kt) or (near and (qs, ks) == (0, 0)):
                        continue
                    i, j = qs * TILES + qt, ks * TILES + kt
                    some = (bound[0, i] <= bound[3, j]) & (bound[1, i] >= bound[2, j])
                    todo[0, count] = i
                    todo[1, count] = j
                    todo[2, count] = i
                    count = count + some.astype(jnp.int32) * here
    for extra in range(3):
        todo[0, count + extra] = 0
        todo[1, count + extra] = 0
        todo[2, count + extra] = sources * TILES
    last = (((1,), (1,)), ((), ()))
    first = (((0,), (0,)), ((), ()))

    def rows_of(tile):
        start = tile * TILE + (tile // TILES) * SEG_ROWS
        return pl.ds(pl.multiple_of(start, SEG_ROWS), TILE), pl.ds(pl.multiple_of(tile * TILE, TILE), TILE)

    def score(n, w_out, d_out):
        qt, kt = todo[0, n], todo[1, n]
        (q_at, _), (k_at, k_flat) = rows_of(qt), rows_of(kt)
        s = lax.dot_general(k[k_at, 0:128], q[q_at, 0:128], last, preferred_element_type=F32)
        p = lax.dot_general(k[k_at, 128:256], q[q_at, 128:256], last, preferred_element_type=F32)
        mask_at = pl.ds(pl.multiple_of(todo[2, n] * TILE, TILE), TILE)
        allowed = col_k[k_flat, 0:1] == row_q[:, mask_at]
        if own:
            ahead = (qt - kt) * TILE
            allowed = allowed & (
                lax.broadcasted_iota(jnp.int32, (TILE, TILE), 1) + ahead
                >= lax.broadcasted_iota(jnp.int32, (TILE, TILE), 0)
            )
        y = jnp.where(allowed, s * HALF_SCALE, -64.0)
        t = jnp.tanh(y)
        u = 1.0 + t
        w = y * u
        d_out[...] = (p * (u + w * (1.0 - t))).astype(BF16)
        w_out[...] = w.astype(BF16)

    def gather(n, w_in, d_in):
        (q_at, q_flat), (k_at, k_flat) = rows_of(todo[0, n]), rows_of(todo[1, n])
        dv[k_flat, :] += jnp.dot(w_in[...], q[q_at, 128:256], preferred_element_type=F32)
        dk[k_flat, :] += jnp.dot(d_in[...], q[q_at, 0:128], preferred_element_type=F32)
        dq[q_flat, :] += lax.dot_general(d_in[...], k[k_at, 0:128], first, preferred_element_type=F32)

    @pl.when(count > 0)
    def _():
        score(0, w0, d0)

        def two(j, carry):
            n = 2 * j
            score(n + 1, w1, d1)
            gather(n, w0, d0)
            score(n + 2, w0, d0)
            gather(n + 1, w1, d1)
            return carry

        lax.fori_loop(0, (count + 1) // 2, two, 0)

    for i in range(sources):
        at = slice(i * PAIR, (i + 1) * PAIR)
        dq_out, dkv_out = outs[i], outs[sources + i]
        dq_out[...] = (dq[at] * HALF_SCALE).astype(dq_out.dtype)
        dkv_out[:, 0:128] = (dk[at] * HALF_SCALE).astype(dkv_out.dtype)
        dkv_out[:, 128:256] = dv[at].astype(dkv_out.dtype)


def pairs(kind, queries, keys, types, area):
    sources = len(queries)
    anywhere = pl.BlockSpec(memory_space=pl.ANY)
    rows = sources * PAIR
    slots = sources * TILES
    return pl.pallas_call(
        lambda *refs: pairs_kernel(kind, sources, *refs),
        in_specs=[anywhere] * (2 * sources),
        out_specs=[VMEM] * (2 * sources),
        out_shape=[jax.ShapeDtypeStruct((PAIR, 128), t) for t in types]
        + [jax.ShapeDtypeStruct((PAIR, 256), t) for t in types],
        scratch_shapes=[
            pltpu.VMEM((rows + sources * SEG_ROWS, 256), BF16),
            pltpu.VMEM((rows + sources * SEG_ROWS, 256), BF16),
            pltpu.VMEM((rows, 128), F32),
            pltpu.VMEM((rows, 128), F32),
            pltpu.VMEM((rows, 128), F32),
            pltpu.VMEM((1, rows + TILE), F32),
            pltpu.VMEM((rows, 128), F32),
            pltpu.SMEM((4, slots), F32),
            pltpu.SMEM((4,), jnp.int32),
            pltpu.SMEM((3, slots * slots + 4), jnp.int32),
            pltpu.VMEM((TILE, TILE), BF16),
            pltpu.VMEM((TILE, TILE), BF16),
            pltpu.VMEM((TILE, TILE), BF16),
            pltpu.VMEM((TILE, TILE), BF16),
            pltpu.SemaphoreType.DMA((2 * sources,)),
        ],
        compiler_params=params(36),
        cost_estimate=cost(20 * area * 128, area, 8 * rows * 256),
        name="pairs_" + kind,
    )(*queries, *keys)


def project_kernel(place, mine, other, gate_grad, weights, out1, out2, out3, own):
    core, x = place[0], place[1]
    a = mine[...]
    b = other[...]
    first = core == 0
    blocks = []
    for p in range(3):
        cols = slice(p * 128, (p + 1) * 128)
        blocks.append(jnp.where(first, a[:, cols], b[:, cols]))
        blocks.append(jnp.where(first, b[:, cols], a[:, cols]))
    for step, out in ((1, out1), (2, out2), (3, out3), (4, own)):
        dest = lax.rem(x + step, 4)
        ds = pl.ds(pl.multiple_of(dest * 256, 256), 256)
        acc = lax.dot_general(gate_grad[...], weights[3, ds, :], (((1,), (1,)), ((), ())),
                              preferred_element_type=F32)
        for p in range(3):
            left = jnp.concatenate([blocks[2 * p], blocks[2 * p + 1]], axis=1)
            acc += lax.dot_general(left, weights[p, ds, :], (((1,), (1,)), ((), ())),
                                   preferred_element_type=F32)
        out[...] = acc.astype(out.dtype)


def project(place, mine, other, gate_grad, weights):
    part = jax.ShapeDtypeStruct((ROWS, 256), BF16)
    return pl.pallas_call(
        project_kernel,
        in_specs=[SMEM, VMEM, VMEM, VMEM, VMEM],
        out_specs=[VMEM] * 4,
        out_shape=[part, part, part, jax.ShapeDtypeStruct((ROWS, 256), F32)],
        compiler_params=params(24),
        cost_estimate=cost(2 * ROWS * 1024 * 1024, 0, 8 * ROWS * 1024),
        name="project",
    )(place, mine, other, gate_grad, weights)


def per_device(queries, key_rows, value_rows, attn_out, gate_pre, out_grad, segments, projections):
    core = lax.axis_index("seq") % 2
    head = lax.axis_index("head")
    core_at = core.reshape(1).astype(jnp.int32)
    keep, send, gate_grad = prepare(
        core_at, queries, key_rows, value_rows, attn_out, gate_pre, out_grad
    )
    users = (segments + 1).astype(BF16)
    recv = swap(send)
    users_recv = swap(users)
    front = core == 0

    def in_order(kept, received):
        return jnp.concatenate([jnp.where(front, kept, received), jnp.where(front, received, kept)])

    seg = in_order(users, users_recv).reshape(PAIR // 256, 256)
    seg = jnp.pad(seg, ((0, SEG_ROWS - PAIR // 256), (0, 0)))
    query = jnp.concatenate([in_order(keep[:, :256], recv[:, :256]), seg])
    key = jnp.concatenate([in_order(keep[:, 256:], recv[:, 256:]), seg])
    query_next, key_prev = shift(query, -2), shift(key, 2)
    dq0, dkv0 = pairs("own", [query], [key], [F32], PAIR * PAIR // 2)
    query, query_next, key_prev, dq0 = lax.optimization_barrier((query, query_next, key_prev, dq0))
    query_far = shift(query, -6)
    dq1, dq_next, dkv1, dkv_prev = pairs(
        "near", [query, query_next], [key, key_prev], [F32, BF16], PAIR * PAIR
    )
    dkv_back, dq_back = shift(dkv_prev, -2), shift(dq_next, 2)
    query_far, dq_next = lax.optimization_barrier((query_far, dq_next))
    dq_far, dkv2 = pairs("far", [query_far], [key], [BF16], PAIR * PAIR // 4)
    far_back = shift(dq_far, 6)
    total = lambda *terms: sum(t.astype(F32) for t in terms).astype(BF16)
    dq = total(dq0, dq1, dq_back, far_back)
    dkv = total(dkv0, dkv1, dkv2, dkv_back)
    grads = jnp.concatenate([dq, dkv], axis=1)
    mine = jnp.where(front, grads[:ROWS], grads[ROWS:])
    other = swap(jnp.where(front, grads[ROWS:], grads[:ROWS]))
    place = jnp.stack([core, head]).astype(jnp.int32)
    part1, part2, part3, own = project(place, mine, other, gate_grad, projections)
    turn = lambda block, by: lax.ppermute(block, "head", [(i, (i + by) % 4) for i in range(4)])
    result = own + turn(part1, 1).astype(F32) + turn(part2, 2).astype(F32) + turn(part3, 3).astype(F32)
    return result.astype(BF16)


def solution(mesh):
    return jax.shard_map(
        per_device,
        mesh=mesh,
        in_specs=(
            P("seq", "head"),
            P("seq", "head"),
            P("seq", "head"),
            P("seq", "head"),
            P("seq", "head"),
            P("seq", "head"),
            P("seq"),
            P(None, None, "head"),
        ),
        out_specs=P("seq", "head"),
        check_vma=False,
    )
```

```python
import jax
import jax.numpy as jnp
from jax import lax
from jax.experimental import pallas as pl
from jax.experimental.pallas import tpu as pltpu
from jax.sharding import PartitionSpec as P

HEAD_DIM = 128
ROWS = 1024
PAIR = 2 * ROWS
SEG_ROWS = 16
TILE = 512
TILES = PAIR // TILE
HALF_SCALE = 0.5 * HEAD_DIM ** (-0.5)
VMEM = pl.BlockSpec(memory_space=pltpu.VMEM)
SMEM = pl.BlockSpec(memory_space=pltpu.SMEM)
BF16, F32 = jnp.bfloat16, jnp.float32


def cost(flops, transcendentals, size):
    return pl.CostEstimate(flops=flops, transcendentals=transcendentals, bytes_accessed=size)


def params(mib):
    return pltpu.CompilerParams(vmem_limit_bytes=mib * 2**20)


def shift(block, distance):
    devices = range(lax.axis_size("seq"))
    return lax.ppermute(block, "seq", [(i, i + distance) for i in devices if i + distance in devices])


def swap(block):
    return lax.ppermute(block, "seq", [(i, i ^ 1) for i in range(lax.axis_size("seq"))])


def silu_slope(v):
    sigma = jax.nn.sigmoid(v)
    return sigma * (1.0 + v * (1.0 - sigma))


def prepare_kernel(core, q, k, v, o, gate, grad, keep, send, gate_grad):
    for slot, out in ((0, keep), (1, send)):
        head = core[0] if slot == 0 else 1 - core[0]
        cols = pl.ds(pl.multiple_of(head * HEAD_DIM, HEAD_DIM), HEAD_DIM)
        saved = o[:, cols].astype(F32)
        centred = saved - jnp.mean(saved, axis=-1, keepdims=True)
        inverse = lax.rsqrt(jnp.mean(centred * centred, axis=-1, keepdims=True) + 1e-06)
        normed = centred * inverse
        gate_in = gate[:, cols].astype(F32)
        grad_in = grad[:, cols].astype(F32)
        gate_grad[:, cols] = (grad_in * normed * silu_slope(gate_in)).astype(BF16)
        g = grad_in * jax.nn.silu(gate_in)
        attn_grad = inverse * (
            g
            - jnp.mean(g, axis=-1, keepdims=True)
            - normed * jnp.mean(g * normed, axis=-1, keepdims=True)
        )
        out[:, 0:128] = q[:, cols]
        out[:, 128:256] = attn_grad.astype(BF16)
        out[:, 256:384] = k[:, cols]
        out[:, 384:512] = v[:, cols]


def prepare(core, *arrays):
    rows = 256
    wide = pl.BlockSpec((rows, 2 * HEAD_DIM), lambda i, c: (i, 0))
    packed = pl.BlockSpec((rows, 4 * HEAD_DIM), lambda i, c: (i, 0))
    return pl.pallas_call(
        prepare_kernel,
        grid_spec=pltpu.PrefetchScalarGridSpec(
            num_scalar_prefetch=1,
            grid=(ROWS // rows,),
            in_specs=[wide] * 6,
            out_specs=[packed, packed, wide],
        ),
        out_shape=[
            jax.ShapeDtypeStruct((ROWS, 4 * HEAD_DIM), BF16),
            jax.ShapeDtypeStruct((ROWS, 4 * HEAD_DIM), BF16),
            jax.ShapeDtypeStruct((ROWS, 2 * HEAD_DIM), BF16),
        ],
        compiler_params=params(60),
        cost_estimate=cost(30 * ROWS * 256, 2 * ROWS * 256, 11 * ROWS * 512),
        name="prepare",
    )(core, *arrays)


def pairs_kernel(own, *refs):
    sources = 1
    q_in, k_in = refs[:sources], refs[sources:2 * sources]
    outs = refs[2 * sources:4 * sources]
    q, k, dq, dk, dv, row_q, col_k, bound, todo, w0, d0, w1, d1, sem = refs[4 * sources:]
    wide = PAIR + SEG_ROWS
    copies = []
    for i in range(sources):
        at = pl.ds(i * wide, wide)
        copies.append(pltpu.make_async_copy(q_in[i], q.at[at], sem.at[2 * i]))
        copies.append(pltpu.make_async_copy(k_in[i], k.at[at], sem.at[2 * i + 1]))
    for copy in copies:
        copy.start()
    dq[...] = jnp.zeros_like(dq)
    dk[...] = jnp.zeros_like(dk)
    dv[...] = jnp.zeros_like(dv)
    for copy in copies:
        copy.wait()
    blocks = PAIR // 256
    for i in range(sources):
        at = slice(i * wide + PAIR, (i + 1) * wide)
        users_q, users_k = q[at].astype(F32), k[at].astype(F32)
        for r in range(blocks):
            start = i * PAIR + r * 256
            row_q[:, start:start + 256] = users_q[r:r + 1]
        padded = jnp.concatenate([users_k, jnp.zeros((128 - SEG_ROWS, 256), F32)])
        for half in range(2):
            turned = jnp.transpose(padded[:, half * 128:half * 128 + 128])
            for r in range(blocks):
                start = i * PAIR + r * 256 + half * 128
                col_k[start:start + 128] = jnp.broadcast_to(turned[:, r:r + 1], (128, 128))
        for b in range(TILES):
            rows = slice(b * TILE // 256, (b + 1) * TILE // 256)
            bound[0, i * TILES + b] = jnp.min(users_q[rows])
            bound[1, i * TILES + b] = jnp.max(users_q[rows])
            bound[2, i * TILES + b] = jnp.min(users_k[rows])
            bound[3, i * TILES + b] = jnp.max(users_k[rows])
    row_q[:, sources * PAIR:] = jnp.full((1, TILE), -1.0, F32)

    count = jnp.int32(0)
    for qs in range(sources):
        for ks in range(sources):
            for kt in range(TILES):
                for qt in range(TILES):
                    if own and qt < kt:
                        continue
                    i, j = qs * TILES + qt, ks * TILES + kt
                    some = (bound[0, i] <= bound[3, j]) & (bound[1, i] >= bound[2, j])
                    todo[0, count] = i
                    todo[1, count] = j
                    todo[2, count] = i
                    count = count + some.astype(jnp.int32)
    for extra in range(3):
        todo[0, count + extra] = 0
        todo[1, count + extra] = 0
        todo[2, count + extra] = sources * TILES
    last = (((1,), (1,)), ((), ()))
    first = (((0,), (0,)), ((), ()))

    def rows_of(tile):
        start = tile * TILE + (tile // TILES) * SEG_ROWS
        return pl.ds(pl.multiple_of(start, SEG_ROWS), TILE), pl.ds(pl.multiple_of(tile * TILE, TILE), TILE)

    def score(n, w_out, d_out):
        qt, kt = todo[0, n], todo[1, n]
        (q_at, _), (k_at, k_flat) = rows_of(qt), rows_of(kt)
        s = lax.dot_general(k[k_at, 0:128], q[q_at, 0:128], last, preferred_element_type=F32)
        p = lax.dot_general(k[k_at, 128:256], q[q_at, 128:256], last, preferred_element_type=F32)
        mask_at = pl.ds(pl.multiple_of(todo[2, n] * TILE, TILE), TILE)
        allowed = col_k[k_flat, 0:1] == row_q[:, mask_at]
        if own:
            ahead = (qt - kt) * TILE
            allowed = allowed & (
                lax.broadcasted_iota(jnp.int32, (TILE, TILE), 1) + ahead
                >= lax.broadcasted_iota(jnp.int32, (TILE, TILE), 0)
            )
        y = jnp.where(allowed, s * HALF_SCALE, -64.0)
        t = jnp.tanh(y)
        u = 1.0 + t
        w = y * u
        d_out[...] = (p * (u + w * (1.0 - t))).astype(BF16)
        w_out[...] = w.astype(BF16)

    def gather(n, w_in, d_in):
        (q_at, q_flat), (k_at, k_flat) = rows_of(todo[0, n]), rows_of(todo[1, n])
        dv[k_flat, :] += jnp.dot(w_in[...], q[q_at, 128:256], preferred_element_type=F32)
        dk[k_flat, :] += jnp.dot(d_in[...], q[q_at, 0:128], preferred_element_type=F32)
        dq[q_flat, :] += lax.dot_general(d_in[...], k[k_at, 0:128], first, preferred_element_type=F32)

    @pl.when(count > 0)
    def _():
        score(0, w0, d0)

        def two(j, carry):
            n = 2 * j
            score(n + 1, w1, d1)
            gather(n, w0, d0)
            score(n + 2, w0, d0)
            gather(n + 1, w1, d1)
            return carry

        lax.fori_loop(0, (count + 1) // 2, two, 0)

    for i in range(sources):
        at = slice(i * PAIR, (i + 1) * PAIR)
        dq_out, dkv_out = outs[i], outs[sources + i]
        dq_out[...] = (dq[at] * HALF_SCALE).astype(dq_out.dtype)
        dkv_out[:, 0:128] = (dk[at] * HALF_SCALE).astype(dkv_out.dtype)
        dkv_out[:, 128:256] = dv[at].astype(dkv_out.dtype)


def pairs(name, query, key, kind, area):
    anywhere = pl.BlockSpec(memory_space=pltpu.HBM)
    return pl.pallas_call(
        lambda *refs: pairs_kernel(name == "pairs_own", *refs),
        in_specs=[anywhere] * 2,
        out_specs=[VMEM] * 2,
        out_shape=[jax.ShapeDtypeStruct((PAIR, 128), kind), jax.ShapeDtypeStruct((PAIR, 256), kind)],
        scratch_shapes=[
            pltpu.VMEM((PAIR + SEG_ROWS, 256), BF16),
            pltpu.VMEM((PAIR + SEG_ROWS, 256), BF16),
            pltpu.VMEM((PAIR, 128), F32),
            pltpu.VMEM((PAIR, 128), F32),
            pltpu.VMEM((PAIR, 128), F32),
            pltpu.VMEM((1, PAIR + TILE), F32),
            pltpu.VMEM((PAIR, 128), F32),
            pltpu.SMEM((4, TILES), F32),
            pltpu.SMEM((3, TILES * TILES + 4), jnp.int32),
            pltpu.VMEM((TILE, TILE), BF16),
            pltpu.VMEM((TILE, TILE), BF16),
            pltpu.VMEM((TILE, TILE), BF16),
            pltpu.VMEM((TILE, TILE), BF16),
            pltpu.SemaphoreType.DMA((2,)),
        ],
        compiler_params=params(28),
        cost_estimate=cost(20 * area * 128, area, 8 * PAIR * 256),
        name=name,
    )(query, key)


def collect_kernel(place, mine, other, dq_same, dq_cross, dkv_same, dkv_cross, gate_grad, weights,
                   left, low, high):
    core, x = place[0], place[1]
    front = core == 0
    for p in range(3):
        cols = slice(p * 128, (p + 1) * 128)
        same, cross = (dq_same, dq_cross) if p == 0 else (dkv_same, dkv_cross)
        part = slice(max(p - 1, 0) * 128, max(p - 1, 0) * 128 + 128)
        a = (mine[:, cols] + same[:, part].astype(F32)).astype(BF16)
        b = (other[:, cols].astype(F32) + cross[:, part].astype(F32)).astype(BF16)
        left[:, p * 256:p * 256 + 128] = jnp.where(front, a, b)
        left[:, p * 256 + 128:p * 256 + 256] = jnp.where(front, b, a)
    left[:, 768:1024] = gate_grad[...]
    far = head_block(left, weights, lax.rem(x + 2, 4)).astype(BF16)
    low[...] = far[:ROWS // 2]
    high[...] = far[ROWS // 2:]


def head_block(left, weights, dest):
    ds = pl.ds(pl.multiple_of(dest * 256, 256), 256)
    acc = None
    for p in range(4):
        term = lax.dot_general(
            left[:, p * 256:p * 256 + 256], weights[p, ds, :], (((1,), (1,)), ((), ())),
            preferred_element_type=F32,
        )
        acc = term if acc is None else acc + term
    return acc


def project_kernel(place, left, weights, after, before, own):
    x = place[1]
    after[...] = head_block(left, weights, lax.rem(x + 1, 4))
    before[...] = head_block(left, weights, lax.rem(x + 3, 4))
    own[...] = head_block(left, weights, x)


def collect(place, *arrays):
    half = jax.ShapeDtypeStruct((ROWS // 2, 256), BF16)
    return pl.pallas_call(
        collect_kernel,
        in_specs=[SMEM] + [VMEM] * 8,
        out_specs=[VMEM] * 3,
        out_shape=[jax.ShapeDtypeStruct((ROWS, 1024), BF16), half, half],
        compiler_params=params(24),
        cost_estimate=cost(2 * ROWS * 1024 * 256, 0, 8 * ROWS * 1024),
        name="collect",
    )(place, *arrays)


def project(place, left, weights):
    return pl.pallas_call(
        project_kernel,
        in_specs=[SMEM, VMEM, VMEM],
        out_specs=[VMEM] * 3,
        out_shape=[jax.ShapeDtypeStruct((ROWS, 256), F32)] * 3,
        compiler_params=params(24),
        cost_estimate=cost(2 * ROWS * 1024 * 768, 0, 8 * ROWS * 1024),
        name="project",
    )(place, left, weights)


def per_device(queries, key_rows, value_rows, attn_out, gate_pre, out_grad, segments, projections):
    core = lax.axis_index("seq") % 2
    head = lax.axis_index("head")
    core_at = core.reshape(1).astype(jnp.int32)
    keep, send, gate_grad = prepare(
        core_at, queries, key_rows, value_rows, attn_out, gate_pre, out_grad
    )
    users = (segments + 1).astype(BF16)
    recv = swap(send)
    users_recv = swap(users)
    front = core == 0

    def in_order(kept, received):
        return jnp.concatenate([jnp.where(front, kept, received), jnp.where(front, received, kept)])

    seg = in_order(users, users_recv).reshape(PAIR // 256, 256)
    seg = jnp.pad(seg, ((0, SEG_ROWS - PAIR // 256), (0, 0)))
    query = jnp.concatenate([in_order(keep[:, :256], recv[:, :256]), seg])
    key = jnp.concatenate([in_order(keep[:, 256:], recv[:, 256:]), seg])
    query_next, key_prev = shift(query, -2), shift(key, 2)
    dq0, dkv0 = pairs("pairs_own", query, key, F32, PAIR * PAIR // 2)
    query_next, key_prev, dq0 = lax.optimization_barrier((query_next, key_prev, dq0))
    query_far = shift(query_next, -2)
    dq2, dkv2 = pairs("pairs_two", query_next, key_prev, BF16, PAIR * PAIR // 2)
    query_far, dq2 = lax.optimization_barrier((query_far, dq2))
    dq3, dkv3 = pairs("pairs_three", query_far, key_prev, BF16, PAIR * PAIR // 8)

    def total(*terms):
        return sum(t.astype(F32) for t in terms)

    def halves(block):
        return jnp.where(front, block[:ROWS], block[ROWS:]), jnp.where(front, block[ROWS:], block[:ROWS])

    def give(block, distance):
        same, cross = halves(block.astype(BF16))
        devices = range(lax.axis_size("seq"))
        route = [(i, (i + distance) ^ 1) for i in devices if i + distance in devices]
        return shift(same, distance), lax.ppermute(cross, "seq", route)

    dkv_same, dkv_cross = give(total(dkv2, dkv3), -2)
    dq3_next = shift(dq3, 2)
    query_next, key, dkv3, dq3 = lax.optimization_barrier((query_next, key, dkv3, dq3))
    dq1, dkv1 = pairs("pairs_one", query_next, key, BF16, PAIR * PAIR)
    dq_same, dq_cross = give(total(dq1, dq2, dq3_next), 2)
    mine, other = halves(jnp.concatenate([dq0, total(dkv0, dkv1)], axis=1))
    other = swap(other.astype(BF16))
    place = jnp.stack([core, head]).astype(jnp.int32)
    left, low, high = collect(
        place, mine, other, dq_same, dq_cross, dkv_same, dkv_cross, gate_grad, projections
    )

    def turn(block, by):
        return lax.ppermute(block, "head", [(i, (i + by) % 4) for i in range(4)])

    low, high = turn(low, 1), turn(high, -1)
    after, before, result = project(place, left, projections)
    half = ROWS // 2
    after = jnp.concatenate([after[:half] + low.astype(F32), after[half:]]).astype(BF16)
    before = jnp.concatenate([before[:half], before[half:] + high.astype(F32)]).astype(BF16)
    return total(result, turn(after, 1), turn(before, -1)).astype(BF16)


def solution(mesh):
    return jax.shard_map(
        per_device,
        mesh=mesh,
        in_specs=(
            P("seq", "head"),
            P("seq", "head"),
            P("seq", "head"),
            P("seq", "head"),
            P("seq", "head"),
            P("seq", "head"),
            P("seq"),
            P(None, None, "head"),
        ),
        out_specs=P("seq", "head"),
        check_vma=False,
    )
```

```python
import jax
import jax.numpy as jnp
from jax import lax
from jax.experimental import pallas as pl
from jax.experimental.pallas import tpu as pltpu
from jax.sharding import PartitionSpec as P


HEAD_DIM = 128
ROWS = 1024
PAIR = 2 * ROWS
SEG_ROWS = 16
TILE = 512
TILES = PAIR // TILE
HALF_SCALE = 0.5 * HEAD_DIM ** (-0.5)
VMEM = pl.BlockSpec(memory_space=pltpu.VMEM)
SMEM = pl.BlockSpec(memory_space=pltpu.SMEM)
BF16, F32 = jnp.bfloat16, jnp.float32


def cost(flops, transcendentals, size):
    return pl.CostEstimate(flops=flops, transcendentals=transcendentals, bytes_accessed=size)


def params(mib):
    return pltpu.CompilerParams(vmem_limit_bytes=mib * 2**20)


def shift(block, distance):
    devices = range(lax.axis_size("seq"))
    return lax.ppermute(block, "seq", [(i, i + distance) for i in devices if i + distance in devices])


def swap(block):
    return lax.ppermute(block, "seq", [(i, i ^ 1) for i in range(lax.axis_size("seq"))])


def silu_slope(v):
    sigma = jax.nn.sigmoid(v)
    return sigma * (1.0 + v * (1.0 - sigma))


def prepare_kernel(core, q, k, v, o, gate, grad, keep, send, gate_grad):
    for slot, out in ((0, keep), (1, send)):
        head = core[0] if slot == 0 else 1 - core[0]
        cols = pl.ds(pl.multiple_of(head * HEAD_DIM, HEAD_DIM), HEAD_DIM)
        saved = o[:, cols].astype(F32)
        centred = saved - jnp.mean(saved, axis=-1, keepdims=True)
        inverse = lax.rsqrt(jnp.mean(centred * centred, axis=-1, keepdims=True) + 1e-06)
        normed = centred * inverse
        gate_in = gate[:, cols].astype(F32)
        grad_in = grad[:, cols].astype(F32)
        gate_grad[:, cols] = (grad_in * normed * silu_slope(gate_in)).astype(BF16)
        g = grad_in * jax.nn.silu(gate_in)
        attn_grad = inverse * (
            g
            - jnp.mean(g, axis=-1, keepdims=True)
            - normed * jnp.mean(g * normed, axis=-1, keepdims=True)
        )
        out[:, 0:128] = q[:, cols]
        out[:, 128:256] = attn_grad.astype(BF16)
        out[:, 256:384] = k[:, cols]
        out[:, 384:512] = v[:, cols]


def prepare(core, *arrays):
    rows = 256
    wide = pl.BlockSpec((rows, 2 * HEAD_DIM), lambda i, c: (i, 0))
    packed = pl.BlockSpec((rows, 4 * HEAD_DIM), lambda i, c: (i, 0))
    return pl.pallas_call(
        prepare_kernel,
        grid_spec=pltpu.PrefetchScalarGridSpec(
            num_scalar_prefetch=1,
            grid=(ROWS // rows,),
            in_specs=[wide] * 6,
            out_specs=[packed, packed, wide],
        ),
        out_shape=[
            jax.ShapeDtypeStruct((ROWS, 4 * HEAD_DIM), BF16),
            jax.ShapeDtypeStruct((ROWS, 4 * HEAD_DIM), BF16),
            jax.ShapeDtypeStruct((ROWS, 2 * HEAD_DIM), BF16),
        ],
        compiler_params=params(60),
        cost_estimate=cost(30 * ROWS * 256, 2 * ROWS * 256, 11 * ROWS * 512),
        name="prepare",
    )(core, *arrays)


def pairs_kernel(own, *refs):
    sources = 1
    q_in, k_in = refs[:sources], refs[sources:2 * sources]
    outs = refs[2 * sources:4 * sources]
    q, k, dq, dk, dv, row_q, col_k, bound, todo, w0, d0, w1, d1, sem = refs[4 * sources:]
    wide = PAIR + SEG_ROWS
    copies = []
    for i in range(sources):
        at = pl.ds(i * wide, wide)
        copies.append(pltpu.make_async_copy(q_in[i], q.at[at], sem.at[2 * i]))
        copies.append(pltpu.make_async_copy(k_in[i], k.at[at], sem.at[2 * i + 1]))
    for copy in copies:
        copy.start()
    dq[...] = jnp.zeros_like(dq)
    dk[...] = jnp.zeros_like(dk)
    dv[...] = jnp.zeros_like(dv)
    for copy in copies:
        copy.wait()
    blocks = PAIR // 256
    for i in range(sources):
        at = slice(i * wide + PAIR, (i + 1) * wide)
        users_q, users_k = q[at].astype(F32), k[at].astype(F32)
        for r in range(blocks):
            start = i * PAIR + r * 256
            row_q[:, start:start + 256] = users_q[r:r + 1]
        padded = jnp.concatenate([users_k, jnp.zeros((128 - SEG_ROWS, 256), F32)])
        for half in range(2):
            turned = jnp.transpose(padded[:, half * 128:half * 128 + 128])
            for r in range(blocks):
                start = i * PAIR + r * 256 + half * 128
                col_k[start:start + 128] = jnp.broadcast_to(turned[:, r:r + 1], (128, 128))
        for b in range(TILES):
            rows = slice(b * TILE // 256, (b + 1) * TILE // 256)
            bound[0, i * TILES + b] = jnp.min(users_q[rows])
            bound[1, i * TILES + b] = jnp.max(users_q[rows])
            bound[2, i * TILES + b] = jnp.min(users_k[rows])
            bound[3, i * TILES + b] = jnp.max(users_k[rows])
    row_q[:, sources * PAIR:] = jnp.full((1, TILE), -1.0, F32)

    count = jnp.int32(0)
    for qs in range(sources):
        for ks in range(sources):
            for kt in range(TILES):
                for qt in range(TILES):
                    if own and qt < kt:
                        continue
                    i, j = qs * TILES + qt, ks * TILES + kt
                    some = (bound[0, i] <= bound[3, j]) & (bound[1, i] >= bound[2, j])
                    todo[0, count] = i
                    todo[1, count] = j
                    todo[2, count] = i
                    count = count + some.astype(jnp.int32)
    for extra in range(3):
        todo[0, count + extra] = 0
        todo[1, count + extra] = 0
        todo[2, count + extra] = sources * TILES
    last = (((1,), (1,)), ((), ()))
    first = (((0,), (0,)), ((), ()))

    def rows_of(tile):
        start = tile * TILE + (tile // TILES) * SEG_ROWS
        return pl.ds(pl.multiple_of(start, SEG_ROWS), TILE), pl.ds(pl.multiple_of(tile * TILE, TILE), TILE)

    def score(n, w_out, d_out):
        qt, kt = todo[0, n], todo[1, n]
        (q_at, _), (k_at, k_flat) = rows_of(qt), rows_of(kt)
        s = lax.dot_general(k[k_at, 0:128], q[q_at, 0:128], last, preferred_element_type=F32)
        p = lax.dot_general(k[k_at, 128:256], q[q_at, 128:256], last, preferred_element_type=F32)
        mask_at = pl.ds(pl.multiple_of(todo[2, n] * TILE, TILE), TILE)
        allowed = col_k[k_flat, 0:1] == row_q[:, mask_at]
        if own:
            ahead = (qt - kt) * TILE
            allowed = allowed & (
                lax.broadcasted_iota(jnp.int32, (TILE, TILE), 1) + ahead
                >= lax.broadcasted_iota(jnp.int32, (TILE, TILE), 0)
            )
        y = jnp.where(allowed, s * HALF_SCALE, -64.0)
        t = jnp.tanh(y)
        u = 1.0 + t
        w = y * u
        d_out[...] = (p * (u + w * (1.0 - t))).astype(BF16)
        w_out[...] = w.astype(BF16)

    def gather(n, w_in, d_in):
        (q_at, q_flat), (k_at, k_flat) = rows_of(todo[0, n]), rows_of(todo[1, n])
        dv[k_flat, :] += jnp.dot(w_in[...], q[q_at, 128:256], preferred_element_type=F32)
        dk[k_flat, :] += jnp.dot(d_in[...], q[q_at, 0:128], preferred_element_type=F32)
        dq[q_flat, :] += lax.dot_general(d_in[...], k[k_at, 0:128], first, preferred_element_type=F32)

    @pl.when(count > 0)
    def _():
        score(0, w0, d0)

        def two(j, carry):
            n = 2 * j
            score(n + 1, w1, d1)
            gather(n, w0, d0)
            score(n + 2, w0, d0)
            gather(n + 1, w1, d1)
            return carry

        lax.fori_loop(0, (count + 1) // 2, two, 0)

    for i in range(sources):
        at = slice(i * PAIR, (i + 1) * PAIR)
        dq_out, dkv_out = outs[i], outs[sources + i]
        dq_out[...] = (dq[at] * HALF_SCALE).astype(dq_out.dtype)
        dkv_out[:, 0:128] = (dk[at] * HALF_SCALE).astype(dkv_out.dtype)
        dkv_out[:, 128:256] = dv[at].astype(dkv_out.dtype)


def pairs(name, query, key, kind, area):
    anywhere = pl.BlockSpec(memory_space=pltpu.HBM)
    return pl.pallas_call(
        lambda *refs: pairs_kernel(name == "pairs_own", *refs),
        in_specs=[anywhere] * 2,
        out_specs=[VMEM] * 2,
        out_shape=[jax.ShapeDtypeStruct((PAIR, 128), kind), jax.ShapeDtypeStruct((PAIR, 256), kind)],
        scratch_shapes=[
            pltpu.VMEM((PAIR + SEG_ROWS, 256), BF16),
            pltpu.VMEM((PAIR + SEG_ROWS, 256), BF16),
            pltpu.VMEM((PAIR, 128), F32),
            pltpu.VMEM((PAIR, 128), F32),
            pltpu.VMEM((PAIR, 128), F32),
            pltpu.VMEM((1, PAIR + TILE), F32),
            pltpu.VMEM((PAIR, 128), F32),
            pltpu.SMEM((4, TILES), F32),
            pltpu.SMEM((3, TILES * TILES + 4), jnp.int32),
            pltpu.VMEM((TILE, TILE), BF16),
            pltpu.VMEM((TILE, TILE), BF16),
            pltpu.VMEM((TILE, TILE), BF16),
            pltpu.VMEM((TILE, TILE), BF16),
            pltpu.SemaphoreType.DMA((2,)),
        ],
        compiler_params=params(28),
        cost_estimate=cost(20 * area * 128, area, 8 * PAIR * 256),
    )(query, key)


def collect_kernel(place, mine, other, far_same, far_cross, gate_grad, weights,
                   left, low, high):
    core, x = place[0], place[1]
    front = core == 0
    for p in range(3):
        cols = slice(p * 128, (p + 1) * 128)
        a, b = mine[:, cols], other[:, cols].astype(F32)
        if p == 0:
            a, b = a + far_same[...].astype(F32), b + far_cross[...].astype(F32)
        a, b = a.astype(BF16), b.astype(BF16)
        left[:, p * 256:p * 256 + 128] = jnp.where(front, a, b)
        left[:, p * 256 + 128:p * 256 + 256] = jnp.where(front, b, a)
    left[:, 768:1024] = gate_grad[...]
    far = head_block(left, weights, lax.rem(x + 2, 4)).astype(BF16)
    low[...] = far[:ROWS // 2]
    high[...] = far[ROWS // 2:]


def head_block(left, weights, dest):
    ds = pl.ds(pl.multiple_of(dest * 256, 256), 256)
    acc = None
    for p in range(4):
        term = lax.dot_general(
            left[:, p * 256:p * 256 + 256], weights[p, ds, :], (((1,), (1,)), ((), ())),
            preferred_element_type=F32,
        )
        acc = term if acc is None else acc + term
    return acc


def project_kernel(place, left, weights, after, before, own):
    x = place[1]
    after[...] = head_block(left, weights, lax.rem(x + 1, 4))
    before[...] = head_block(left, weights, lax.rem(x + 3, 4))
    own[...] = head_block(left, weights, x)


def collect(place, *arrays):
    half = jax.ShapeDtypeStruct((ROWS // 2, 256), BF16)
    return pl.pallas_call(
        collect_kernel,
        in_specs=[SMEM] + [VMEM] * 6,
        out_specs=[VMEM] * 3,
        out_shape=[jax.ShapeDtypeStruct((ROWS, 1024), BF16), half, half],
        compiler_params=params(24),
        cost_estimate=cost(2 * ROWS * 1024 * 256, 0, 8 * ROWS * 1024),
        name="collect",
    )(place, *arrays)


def project(place, left, weights):
    return pl.pallas_call(
        project_kernel,
        in_specs=[SMEM, VMEM, VMEM],
        out_specs=[VMEM] * 3,
        out_shape=[jax.ShapeDtypeStruct((ROWS, 256), F32)] * 3,
        compiler_params=params(24),
        cost_estimate=cost(2 * ROWS * 1024 * 768, 0, 8 * ROWS * 1024),
        name="project",
    )(place, left, weights)


def compute(queries, key_rows, value_rows, attn_out, gate_pre, out_grad, segments, projections):
    core = lax.axis_index("seq") % 2
    head = lax.axis_index("head")
    core_at = core.reshape(1).astype(jnp.int32)
    keep, send, gate_grad = prepare(
        core_at, queries, key_rows, value_rows, attn_out, gate_pre, out_grad
    )
    users = (segments + 1).astype(BF16)
    recv = swap(send)
    users_recv = swap(users)
    front = core == 0

    def in_order(kept, received):
        return jnp.concatenate([jnp.where(front, kept, received), jnp.where(front, received, kept)])

    seg = in_order(users, users_recv).reshape(PAIR // 256, 256)
    seg = jnp.pad(seg, ((0, SEG_ROWS - PAIR // 256), (0, 0)))
    query = jnp.concatenate([in_order(keep[:, :256], recv[:, :256]), seg])
    key = jnp.concatenate([in_order(keep[:, 256:], recv[:, 256:]), seg])
    query_next = shift(query, -2)
    key_prev = shift(key, 2)
    dq0, dkv0 = pairs("pairs_own", query, key, F32, PAIR * PAIR // 2)
    query, query_next, key_prev, dq0 = lax.optimization_barrier((query, query_next, key_prev, dq0))
    query_far = shift(query, -6)

    def total(*terms):
        return sum(t.astype(F32) for t in terms)

    def halves(block):
        return jnp.where(front, block[:ROWS], block[ROWS:]), jnp.where(front, block[ROWS:], block[:ROWS])

    dq2, dkv2 = pairs("pairs_two", query_next, key_prev, BF16, PAIR * PAIR // 2)
    dkv_back = shift(dkv2, -2)
    query_next, dq2 = lax.optimization_barrier((query_next, dq2))
    dq1, dkv1 = pairs("pairs_one", query_next, key, BF16, PAIR * PAIR)
    dq_back = shift(total(dq1, dq2).astype(BF16), 2)
    query_far, dq1 = lax.optimization_barrier((query_far, dq1))
    dq3, dkv3 = pairs("pairs_three", query_far, key, BF16, PAIR * PAIR // 8)
    same, cross = halves(dq3)
    route = [(i, (i + 6) ^ 1) for i in range(lax.axis_size("seq") - 6)]
    far_same = shift(same, 6)
    far_cross = lax.ppermute(cross, "seq", route)
    grads = jnp.concatenate([total(dq0, dq_back), total(dkv0, dkv1, dkv3, dkv_back)], axis=1)
    mine, other = halves(grads)
    other = swap(other.astype(BF16))
    place = jnp.stack([core, head]).astype(jnp.int32)
    left, low, high = collect(place, mine, other, far_same, far_cross, gate_grad, projections)

    def turn(block, by):
        return lax.ppermute(block, "head", [(i, (i + by) % 4) for i in range(4)])

    low, high = turn(low, 1), turn(high, -1)
    after, before, result = project(place, left, projections)
    half = ROWS // 2
    after = jnp.concatenate([after[:half] + low.astype(F32), after[half:]]).astype(BF16)
    before = jnp.concatenate([before[:half], before[half:] + high.astype(F32)]).astype(BF16)
    return total(result, turn(after, 1), turn(before, -1)).astype(BF16)


def solution(mesh):
    split = P("seq", "head")
    return jax.shard_map(
        compute,
        mesh=mesh,
        in_specs=(split,) * 6 + (P("seq"), P(None, None, "head")),
        out_specs=split,
        check_vma=False,
    )
```

```python
import jax
import jax.numpy as jnp
from jax import lax
from jax.experimental import pallas as pl
from jax.experimental.pallas import tpu as pltpu
from jax.sharding import PartitionSpec as P


HEAD_DIM = 128
ROWS = 1024
PAIR = 2 * ROWS
SEG_ROWS = 16
TILE = 512
TILES = PAIR // TILE
HALF_SCALE = 0.5 * HEAD_DIM ** (-0.5)
VMEM = pl.BlockSpec(memory_space=pltpu.VMEM)
SMEM = pl.BlockSpec(memory_space=pltpu.SMEM)
BF16, F32 = jnp.bfloat16, jnp.float32


def cost(flops, transcendentals, size):
    return pl.CostEstimate(flops=flops, transcendentals=transcendentals, bytes_accessed=size)


def params(mib):
    return pltpu.CompilerParams(vmem_limit_bytes=mib * 2**20)


def shift(block, distance):
    devices = range(lax.axis_size("seq"))
    return lax.ppermute(block, "seq", [(i, i + distance) for i in devices if i + distance in devices])


def swap(block):
    return lax.ppermute(block, "seq", [(i, i ^ 1) for i in range(lax.axis_size("seq"))])


def silu_slope(v):
    sigma = jax.nn.sigmoid(v)
    return sigma * (1.0 + v * (1.0 - sigma))


def split_kernel(core, k, v, keep, send):
    for slot, out in ((0, keep), (1, send)):
        head = core[0] if slot == 0 else 1 - core[0]
        cols = pl.ds(pl.multiple_of(head * HEAD_DIM, HEAD_DIM), HEAD_DIM)
        out[:, 0:128] = k[:, cols]
        out[:, 128:256] = v[:, cols]


def prepare_kernel(core, q, o, gate, grad, keep, send, gate_grad):
    for slot, out in ((0, keep), (1, send)):
        head = core[0] if slot == 0 else 1 - core[0]
        cols = pl.ds(pl.multiple_of(head * HEAD_DIM, HEAD_DIM), HEAD_DIM)
        saved = o[:, cols].astype(F32)
        centred = saved - jnp.mean(saved, axis=-1, keepdims=True)
        inverse = lax.rsqrt(jnp.mean(centred * centred, axis=-1, keepdims=True) + 1e-06)
        normed = centred * inverse
        gate_in = gate[:, cols].astype(F32)
        grad_in = grad[:, cols].astype(F32)
        gate_grad[:, cols] = (grad_in * normed * silu_slope(gate_in)).astype(BF16)
        g = grad_in * jax.nn.silu(gate_in)
        attn_grad = inverse * (
            g
            - jnp.mean(g, axis=-1, keepdims=True)
            - normed * jnp.mean(g * normed, axis=-1, keepdims=True)
        )
        out[:, 0:128] = q[:, cols]
        out[:, 128:256] = attn_grad.astype(BF16)


def by_rows(kernel, outputs, core, *arrays):
    rows = 256
    wide = pl.BlockSpec((rows, 2 * HEAD_DIM), lambda i, c: (i, 0))
    return pl.pallas_call(
        kernel,
        grid_spec=pltpu.PrefetchScalarGridSpec(
            num_scalar_prefetch=1,
            grid=(ROWS // rows,),
            in_specs=[wide] * len(arrays),
            out_specs=[wide] * outputs,
        ),
        out_shape=[jax.ShapeDtypeStruct((ROWS, 2 * HEAD_DIM), BF16)] * outputs,
        compiler_params=params(60),
        cost_estimate=cost(30 * ROWS * 256, 2 * ROWS * 256, 8 * ROWS * 512),
    )(core, *arrays)


def pairs_kernel(own, parts, tiles, *refs):
    q_in, k_in, dq_out, dkv_out = refs[:len(parts)], refs[len(parts)], refs[len(parts) + 1], refs[len(parts) + 2]
    q, k, dq, dk, dv, row_q, col_k, bound, todo, w0, d0, w1, d1, sem = refs[len(parts) + 3:]
    copies = [pltpu.make_async_copy(k_in, k, sem.at[0])]
    for ref, moves in zip(q_in, parts):
        for source, target, size in moves:
            copies.append(
                pltpu.make_async_copy(
                    ref.at[pl.ds(source, size)], q.at[pl.ds(target, size)], sem.at[len(copies)]
                )
            )
    for copy in copies:
        copy.start()
    dq[...] = jnp.zeros_like(dq)
    dk[...] = jnp.zeros_like(dk)
    dv[...] = jnp.zeros_like(dv)
    for copy in copies:
        copy.wait()
    blocks = PAIR // 256
    users_q, users_k = q[PAIR:].astype(F32), k[PAIR:].astype(F32)
    padded = jnp.concatenate([users_k, jnp.zeros((128 - SEG_ROWS, 256), F32)])
    for half in range(2):
        turned = jnp.transpose(padded[:, half * 128:half * 128 + 128])
        for r in range(blocks):
            start = r * 256 + half * 128
            col_k[start:start + 128] = jnp.broadcast_to(turned[:, r:r + 1], (128, 128))
    for r in range(blocks):
        row_q[:, r * 256:(r + 1) * 256] = users_q[r:r + 1]
    row_q[:, PAIR:] = jnp.full((1, TILE), -1.0, F32)
    for b in range(TILES):
        rows = slice(b * TILE // 256, (b + 1) * TILE // 256)
        bound[0, b] = jnp.min(users_q[rows])
        bound[1, b] = jnp.max(users_q[rows])
        bound[2, b] = jnp.min(users_k[rows])
        bound[3, b] = jnp.max(users_k[rows])

    count = jnp.int32(0)
    for kt in range(TILES):
        for qt in tiles:
            if own and qt < kt:
                continue
            some = (bound[0, qt] <= bound[3, kt]) & (bound[1, qt] >= bound[2, kt])
            todo[0, count] = qt
            todo[1, count] = kt
            todo[2, count] = qt
            count = count + some.astype(jnp.int32)
    for extra in range(3):
        todo[0, count + extra] = tiles[0]
        todo[1, count + extra] = 0
        todo[2, count + extra] = TILES
    last = (((1,), (1,)), ((), ()))
    first = (((0,), (0,)), ((), ()))

    def rows_of(tile):
        return pl.ds(pl.multiple_of(tile * TILE, TILE), TILE)

    def score(n, w_out, d_out):
        qt, kt = todo[0, n], todo[1, n]
        q_at, k_at = rows_of(qt), rows_of(kt)
        s = lax.dot_general(k[k_at, 0:128], q[q_at, 0:128], last, preferred_element_type=F32)
        p = lax.dot_general(k[k_at, 128:256], q[q_at, 128:256], last, preferred_element_type=F32)
        allowed = col_k[k_at, 0:1] == row_q[:, rows_of(todo[2, n])]
        if own:
            ahead = (qt - kt) * TILE
            allowed = allowed & (
                lax.broadcasted_iota(jnp.int32, (TILE, TILE), 1) + ahead
                >= lax.broadcasted_iota(jnp.int32, (TILE, TILE), 0)
            )
        y = jnp.where(allowed, s * HALF_SCALE, -64.0)
        t = jnp.tanh(y)
        u = 1.0 + t
        w = y * u
        d_out[...] = (p * (u + w * (1.0 - t))).astype(BF16)
        w_out[...] = w.astype(BF16)

    def gather(n, w_in, d_in):
        q_at, k_at = rows_of(todo[0, n]), rows_of(todo[1, n])
        dv[k_at, :] += jnp.dot(w_in[...], q[q_at, 128:256], preferred_element_type=F32)
        dk[k_at, :] += jnp.dot(d_in[...], q[q_at, 0:128], preferred_element_type=F32)
        dq[q_at, :] += lax.dot_general(d_in[...], k[k_at, 0:128], first, preferred_element_type=F32)

    @pl.when(count > 0)
    def _():
        score(0, w0, d0)

        def two(j, carry):
            n = 2 * j
            score(n + 1, w1, d1)
            gather(n, w0, d0)
            score(n + 2, w0, d0)
            gather(n + 1, w1, d1)
            return carry

        lax.fori_loop(0, (count + 1) // 2, two, 0)

    at = slice(tiles[0] * TILE, (tiles[-1] + 1) * TILE)
    dq_out[...] = (dq[at] * HALF_SCALE).astype(dq_out.dtype)
    dkv_out[:, 0:128] = (dk[...] * HALF_SCALE).astype(dkv_out.dtype)
    dkv_out[:, 128:256] = dv[...].astype(dkv_out.dtype)


WHOLE = [(0, 0, PAIR + SEG_ROWS)]
EARLY = [(0, 0, ROWS), (ROWS, PAIR, SEG_ROWS)]
USERS_ONLY = [(ROWS, PAIR, SEG_ROWS)]
LATE = [(0, ROWS, ROWS)]


def pairs(name, queries, parts, key, kind, tiles, area):
    anywhere = pl.BlockSpec(memory_space=pl.ANY)
    return pl.pallas_call(
        lambda *refs: pairs_kernel(name == "pairs_own", parts, tiles, *refs),
        in_specs=[anywhere] * (len(queries) + 1),
        out_specs=[VMEM] * 2,
        out_shape=[
            jax.ShapeDtypeStruct((len(tiles) * TILE, 128), kind),
            jax.ShapeDtypeStruct((PAIR, 256), kind),
        ],
        scratch_shapes=[
            pltpu.VMEM((PAIR + SEG_ROWS, 256), BF16),
            pltpu.VMEM((PAIR + SEG_ROWS, 256), BF16),
            pltpu.VMEM((PAIR, 128), F32),
            pltpu.VMEM((PAIR, 128), F32),
            pltpu.VMEM((PAIR, 128), F32),
            pltpu.VMEM((1, PAIR + TILE), F32),
            pltpu.VMEM((PAIR, 128), F32),
            pltpu.SMEM((4, TILES), F32),
            pltpu.SMEM((3, TILES * TILES + 4), jnp.int32),
            pltpu.VMEM((TILE, TILE), BF16),
            pltpu.VMEM((TILE, TILE), BF16),
            pltpu.VMEM((TILE, TILE), BF16),
            pltpu.VMEM((TILE, TILE), BF16),
            pltpu.SemaphoreType.DMA((4,)),
        ],
        compiler_params=params(28),
        cost_estimate=cost(20 * area * 128, area, 8 * PAIR * 256),
    )(*queries, key)


def collect_kernel(place, mine, other, back_same, back_cross, far_same, far_cross, gate_grad, weights,
                   left, low, high):
    core, x = place[0], place[1]
    front = core == 0
    for p in range(3):
        cols = slice(p * 128, (p + 1) * 128)
        a, b = mine[:, cols], other[:, cols].astype(F32)
        if p == 0:
            a = a + back_same[...].astype(F32) + far_same[...].astype(F32)
            b = b + back_cross[...].astype(F32) + far_cross[...].astype(F32)
        a, b = a.astype(BF16), b.astype(BF16)
        left[:, p * 256:p * 256 + 128] = jnp.where(front, a, b)
        left[:, p * 256 + 128:p * 256 + 256] = jnp.where(front, b, a)
    left[:, 768:1024] = gate_grad[...]
    far = head_block(left, weights, lax.rem(x + 2, 4)).astype(BF16)
    low[...] = far[:ROWS // 2]
    high[...] = far[ROWS // 2:]


def head_block(left, weights, dest):
    ds = pl.ds(pl.multiple_of(dest * 256, 256), 256)
    acc = None
    for p in range(4):
        term = lax.dot_general(
            left[:, p * 256:p * 256 + 256], weights[p, ds, :], (((1,), (1,)), ((), ())),
            preferred_element_type=F32,
        )
        acc = term if acc is None else acc + term
    return acc


def project_kernel(place, left, weights, after, before, own):
    x = place[1]
    after[...] = head_block(left, weights, lax.rem(x + 1, 4))
    before[...] = head_block(left, weights, lax.rem(x + 3, 4))
    own[...] = head_block(left, weights, x)


def collect(place, *arrays):
    half = jax.ShapeDtypeStruct((ROWS // 2, 256), BF16)
    return pl.pallas_call(
        collect_kernel,
        in_specs=[SMEM] + [VMEM] * 8,
        out_specs=[VMEM] * 3,
        out_shape=[jax.ShapeDtypeStruct((ROWS, 1024), BF16), half, half],
        compiler_params=params(24),
        cost_estimate=cost(2 * ROWS * 1024 * 256, 0, 8 * ROWS * 1024),
        name="collect",
    )(place, *arrays)


def project(place, left, weights):
    return pl.pallas_call(
        project_kernel,
        in_specs=[SMEM, VMEM, VMEM],
        out_specs=[VMEM] * 3,
        out_shape=[jax.ShapeDtypeStruct((ROWS, 256), F32)] * 3,
        compiler_params=params(24),
        cost_estimate=cost(2 * ROWS * 1024 * 768, 0, 8 * ROWS * 1024),
        name="project",
    )(place, left, weights)


def compute(queries, key_rows, value_rows, attn_out, gate_pre, out_grad, segments, projections):
    core = lax.axis_index("seq") % 2
    head = lax.axis_index("head")
    front = core == 0
    core_at = core.reshape(1).astype(jnp.int32)

    def in_order(kept, received):
        return jnp.where(front, kept, received), jnp.where(front, received, kept)

    def total(*terms):
        return sum(t.astype(F32) for t in terms)

    def halves(block):
        return in_order(block[:ROWS], block[ROWS:])

    def give(same, cross, distance):
        devices = range(lax.axis_size("seq") - distance)
        same = shift(same, distance)
        cross = lax.ppermute(cross, "seq", [(i, (i + distance) ^ 1) for i in devices])
        return same, cross

    users = (segments + 1).astype(BF16)
    users_recv = swap(users)
    kv_keep, kv_send = by_rows(split_kernel, 2, core_at, key_rows, value_rows)
    kv_recv = swap(kv_send)
    keep, send, gate_grad = by_rows(
        prepare_kernel, 3, core_at, queries, attn_out, gate_pre, out_grad
    )
    recv = swap(send)
    seg = jnp.concatenate(in_order(users, users_recv)).reshape(PAIR // 256, 256)
    seg = jnp.pad(seg, ((0, SEG_ROWS - PAIR // 256), (0, 0)))
    key = jnp.concatenate([*in_order(kv_keep, kv_recv), seg])
    key_prev = shift(key, 2)
    recv, key, seg = lax.optimization_barrier((recv, key, seg))
    low_rows, high_rows = in_order(keep, recv)
    next_a = shift(jnp.concatenate([low_rows, seg]), -2)
    next_b = shift(high_rows, -2)
    query = jnp.concatenate([low_rows, high_rows, seg])
    every, early, late = (0, 1, 2, 3), (0, 1), (2, 3)
    area = PAIR * PAIR
    dq0, dkv0 = pairs("pairs_own", [query], [WHOLE], key, F32, every, area // 2)
    next_a, dq0 = lax.optimization_barrier((next_a, dq0))
    dq1a, dkv1a = pairs("pairs_one", [next_a], [EARLY], key, BF16, early, area // 2)
    query, next_a, next_b, key_prev, dq1a = lax.optimization_barrier(
        (query, next_a, next_b, key_prev, dq1a)
    )
    query_far = shift(query, -6)
    dq2, dkv2 = pairs(
        "pairs_two", [next_a, next_b], [EARLY, LATE], key_prev, BF16, every, area // 2
    )
    dkv_back = shift(dkv2, -2)
    next_b, dq2 = lax.optimization_barrier((next_b, dq2))
    dq1b, dkv1b = pairs(
        "pairs_one", [next_a, next_b], [USERS_ONLY, LATE], key, BF16, late, area // 2
    )
    back = in_order(total(dq1a, dq2[:ROWS]).astype(BF16), total(dq1b, dq2[ROWS:]).astype(BF16))
    back_same, back_cross = give(*back, 2)
    query_far, dq1b = lax.optimization_barrier((query_far, dq1b))
    dq3, dkv3 = pairs("pairs_three", [query_far], [WHOLE], key, BF16, every, area // 8)
    far_same, far_cross = give(*halves(dq3), 6)
    grads = jnp.concatenate([dq0, total(dkv0, dkv1a, dkv1b, dkv3, dkv_back)], axis=1)
    mine, other = halves(grads)
    other = swap(other.astype(BF16))
    place = jnp.stack([core, head]).astype(jnp.int32)
    left, low, high = collect(
        place, mine, other, back_same, back_cross, far_same, far_cross, gate_grad, projections
    )

    def turn(block, by):
        return lax.ppermute(block, "head", [(i, (i + by) % 4) for i in range(4)])

    low, high = turn(low, 1), turn(high, -1)
    after, before, result = project(place, left, projections)
    half = ROWS // 2
    after = jnp.concatenate([after[:half] + low.astype(F32), after[half:]]).astype(BF16)
    before = jnp.concatenate([before[:half], before[half:] + high.astype(F32)]).astype(BF16)
    return total(result, turn(after, 1), turn(before, -1)).astype(BF16)


def solution(mesh):
    split = P("seq", "head")
    return jax.shard_map(
        compute,
        mesh=mesh,
        in_specs=(split,) * 6 + (P("seq"), P(None, None, "head")),
        out_specs=split,
        check_vma=False,
    )
```

```python
import jax
import jax.numpy as jnp
from jax import lax
from jax.experimental import pallas as pl
from jax.experimental.pallas import tpu as pltpu
from jax.sharding import PartitionSpec as P


HEAD_DIM = 128
ROWS = 1024
PAIR = 2 * ROWS
SEG_ROWS = 16
TILE = 512
TILES = PAIR // TILE
HALF_SCALE = 0.5 * HEAD_DIM ** (-0.5)
VMEM = pl.BlockSpec(memory_space=pltpu.VMEM)
SMEM = pl.BlockSpec(memory_space=pltpu.SMEM)
BF16, F32 = jnp.bfloat16, jnp.float32


def cost(flops, transcendentals, size):
    return pl.CostEstimate(flops=flops, transcendentals=transcendentals, bytes_accessed=size)


def params(mib):
    return pltpu.CompilerParams(vmem_limit_bytes=mib * 2**20)


def move(block, target):
    devices = range(lax.axis_size("seq"))
    route = [(i, target(i)) for i in devices if target(i) in devices]
    return lax.ppermute(block, "seq", route)


def shift(block, distance):
    return move(block, lambda i: i + distance)


def swap(block):
    return lax.ppermute(block, "seq", [(i, i ^ 1) for i in range(lax.axis_size("seq"))])


def total(*terms):
    return sum(t.astype(F32) for t in terms)


def silu_slope(v):
    sigma = jax.nn.sigmoid(v)
    return sigma * (1.0 + v * (1.0 - sigma))


def prepare_kernel(core, q, o, gate, grad, keep, send, gate_grad):
    for slot, out in ((0, keep), (1, send)):
        head = core[0] if slot == 0 else 1 - core[0]
        cols = pl.ds(pl.multiple_of(head * HEAD_DIM, HEAD_DIM), HEAD_DIM)
        saved = o[:, cols].astype(F32)
        centred = saved - jnp.mean(saved, axis=-1, keepdims=True)
        inverse = lax.rsqrt(jnp.mean(centred * centred, axis=-1, keepdims=True) + 1e-06)
        normed = centred * inverse
        gate_in = gate[:, cols].astype(F32)
        grad_in = grad[:, cols].astype(F32)
        gate_grad[:, cols] = (grad_in * normed * silu_slope(gate_in)).astype(BF16)
        g = grad_in * jax.nn.silu(gate_in)
        attn_grad = inverse * (
            g
            - jnp.mean(g, axis=-1, keepdims=True)
            - normed * jnp.mean(g * normed, axis=-1, keepdims=True)
        )
        out[:, 0:128] = q[:, cols]
        out[:, 128:256] = attn_grad.astype(BF16)


def by_rows(kernel, outputs, core, *arrays):
    rows = 256
    wide = pl.BlockSpec((rows, 2 * HEAD_DIM), lambda i, c: (i, 0))
    return pl.pallas_call(
        kernel,
        grid_spec=pltpu.PrefetchScalarGridSpec(
            num_scalar_prefetch=1,
            grid=(ROWS // rows,),
            in_specs=[wide] * len(arrays),
            out_specs=[wide] * outputs,
        ),
        out_shape=[jax.ShapeDtypeStruct((ROWS, 2 * HEAD_DIM), BF16)] * outputs,
        compiler_params=params(60),
        cost_estimate=cost(30 * ROWS * 256, 2 * ROWS * 256, 8 * ROWS * 512),
    )(core, *arrays)


def pairs_kernel(own, parts, tiles, *refs):
    q_in, k_in, dq_out, dkv_out = refs[:len(parts)], refs[len(parts)], refs[len(parts) + 1], refs[len(parts) + 2]
    q, k, dq, dk, dv, row_q, col_k, bound, todo, w0, d0, w1, d1, sem = refs[len(parts) + 3:]
    copies = [pltpu.make_async_copy(k_in, k, sem.at[0])]
    for ref, moves in zip(q_in, parts):
        for source, target, size in moves:
            copies.append(
                pltpu.make_async_copy(
                    ref.at[pl.ds(source, size)], q.at[pl.ds(target, size)], sem.at[len(copies)]
                )
            )
    for copy in copies:
        copy.start()
    dq[...] = jnp.zeros_like(dq)
    dk[...] = jnp.zeros_like(dk)
    dv[...] = jnp.zeros_like(dv)
    for copy in copies:
        copy.wait()
    blocks = PAIR // 256
    users_q, users_k = q[PAIR:].astype(F32), k[PAIR:].astype(F32)
    padded = jnp.concatenate([users_k, jnp.zeros((128 - SEG_ROWS, 256), F32)])
    for half in range(2):
        turned = jnp.transpose(padded[:, half * 128:half * 128 + 128])
        for r in range(blocks):
            start = r * 256 + half * 128
            col_k[start:start + 128] = jnp.broadcast_to(turned[:, r:r + 1], (128, 128))
    for r in range(blocks):
        row_q[:, r * 256:(r + 1) * 256] = users_q[r:r + 1]
    row_q[:, PAIR:] = jnp.full((1, TILE), -1.0, F32)
    for b in range(TILES):
        rows = slice(b * TILE // 256, (b + 1) * TILE // 256)
        bound[0, b] = jnp.min(users_q[rows])
        bound[1, b] = jnp.max(users_q[rows])
        bound[2, b] = jnp.min(users_k[rows])
        bound[3, b] = jnp.max(users_k[rows])

    count = jnp.int32(0)
    for kt in range(TILES):
        for qt in tiles:
            if own and qt < kt:
                continue
            some = (bound[0, qt] <= bound[3, kt]) & (bound[1, qt] >= bound[2, kt])
            todo[0, count] = qt
            todo[1, count] = kt
            todo[2, count] = qt
            count = count + some.astype(jnp.int32)
    for extra in range(3):
        todo[0, count + extra] = tiles[0]
        todo[1, count + extra] = 0
        todo[2, count + extra] = TILES
    last = (((1,), (1,)), ((), ()))
    first = (((0,), (0,)), ((), ()))

    def rows_of(tile):
        return pl.ds(pl.multiple_of(tile * TILE, TILE), TILE)

    def score(n, w_out, d_out):
        qt, kt = todo[0, n], todo[1, n]
        q_at, k_at = rows_of(qt), rows_of(kt)
        s = lax.dot_general(k[k_at, 0:128], q[q_at, 0:128], last, preferred_element_type=F32)
        p = lax.dot_general(k[k_at, 128:256], q[q_at, 128:256], last, preferred_element_type=F32)
        allowed = col_k[k_at, 0:1] == row_q[:, rows_of(todo[2, n])]
        if own:
            ahead = (qt - kt) * TILE
            allowed = allowed & (
                lax.broadcasted_iota(jnp.int32, (TILE, TILE), 1) + ahead
                >= lax.broadcasted_iota(jnp.int32, (TILE, TILE), 0)
            )
        y = jnp.where(allowed, s * HALF_SCALE, -64.0)
        t = jnp.tanh(y)
        u = 1.0 + t
        w = y * u
        d_out[...] = (p * (u + w * (1.0 - t))).astype(BF16)
        w_out[...] = w.astype(BF16)

    def gather(n, w_in, d_in):
        q_at, k_at = rows_of(todo[0, n]), rows_of(todo[1, n])
        dv[k_at, :] += jnp.dot(w_in[...], q[q_at, 128:256], preferred_element_type=F32)
        dk[k_at, :] += jnp.dot(d_in[...], q[q_at, 0:128], preferred_element_type=F32)
        dq[q_at, :] += lax.dot_general(d_in[...], k[k_at, 0:128], first, preferred_element_type=F32)

    @pl.when(count > 0)
    def _():
        score(0, w0, d0)

        def two(j, carry):
            n = 2 * j
            score(n + 1, w1, d1)
            gather(n, w0, d0)
            score(n + 2, w0, d0)
            gather(n + 1, w1, d1)
            return carry

        lax.fori_loop(0, (count + 1) // 2, two, 0)

    at = slice(tiles[0] * TILE, (tiles[-1] + 1) * TILE)
    dq_out[...] = (dq[at] * HALF_SCALE).astype(dq_out.dtype)
    dkv_out[:, 0:128] = (dk[...] * HALF_SCALE).astype(dkv_out.dtype)
    dkv_out[:, 128:256] = dv[...].astype(dkv_out.dtype)


WHOLE = [(0, 0, PAIR + SEG_ROWS)]
EARLY = [(0, 0, ROWS), (ROWS, PAIR, SEG_ROWS)]


def pairs(name, queries, parts, key, kind, tiles, area):
    anywhere = pl.BlockSpec(memory_space=pl.ANY)
    return pl.pallas_call(
        lambda *refs: pairs_kernel(name == "pairs_own", parts, tiles, *refs),
        in_specs=[anywhere] * (len(queries) + 1),
        out_specs=[VMEM] * 2,
        out_shape=[
            jax.ShapeDtypeStruct((len(tiles) * TILE, 128), kind),
            jax.ShapeDtypeStruct((PAIR, 256), kind),
        ],
        scratch_shapes=[
            pltpu.VMEM((PAIR + SEG_ROWS, 256), BF16),
            pltpu.VMEM((PAIR + SEG_ROWS, 256), BF16),
            pltpu.VMEM((PAIR, 128), F32),
            pltpu.VMEM((PAIR, 128), F32),
            pltpu.VMEM((PAIR, 128), F32),
            pltpu.VMEM((1, PAIR + TILE), F32),
            pltpu.VMEM((PAIR, 128), F32),
            pltpu.SMEM((4, TILES), F32),
            pltpu.SMEM((3, TILES * TILES + 4), jnp.int32),
            pltpu.VMEM((TILE, TILE), BF16),
            pltpu.VMEM((TILE, TILE), BF16),
            pltpu.VMEM((TILE, TILE), BF16),
            pltpu.VMEM((TILE, TILE), BF16),
            pltpu.SemaphoreType.DMA((4,)),
        ],
        compiler_params=params(28),
        cost_estimate=cost(20 * area * 128, area, 8 * PAIR * 256),
    )(*queries, key)


def collect_kernel(place, mine, other, back_same, back_cross, far_same, far_cross, two_same, two_cross,
                   key_same, key_cross, gate_grad, weights, left, low, high):
    core, x = place[0], place[1]
    front = core == 0
    for p in range(3):
        cols = slice(p * 128, (p + 1) * 128)
        a, b = mine[:, cols], other[:, cols].astype(F32)
        if p == 0:
            a = a + total(back_same[...], far_same[...], two_same[...])
            b = b + total(back_cross[...], far_cross[...], two_cross[...])
        else:
            part = slice((p - 1) * 128, p * 128)
            a, b = a + key_same[:, part].astype(F32), b + key_cross[:, part].astype(F32)
        a, b = a.astype(BF16), b.astype(BF16)
        left[:, p * 256:p * 256 + 128] = jnp.where(front, a, b)
        left[:, p * 256 + 128:p * 256 + 256] = jnp.where(front, b, a)
    left[:, 768:1024] = gate_grad[...]
    far = head_block(left, weights, lax.rem(x + 2, 4)).astype(BF16)
    low[...] = far[:ROWS // 2]
    high[...] = far[ROWS // 2:]


def head_block(left, weights, dest):
    ds = pl.ds(pl.multiple_of(dest * 256, 256), 256)
    acc = None
    for p in range(4):
        term = lax.dot_general(
            left[:, p * 256:p * 256 + 256], weights[p, ds, :], (((1,), (1,)), ((), ())),
            preferred_element_type=F32,
        )
        acc = term if acc is None else acc + term
    return acc


def project_kernel(place, left, weights, after, before, own):
    x = place[1]
    after[...] = head_block(left, weights, lax.rem(x + 1, 4))
    before[...] = head_block(left, weights, lax.rem(x + 3, 4))
    own[...] = head_block(left, weights, x)


def collect(place, *arrays):
    half = jax.ShapeDtypeStruct((ROWS // 2, 256), BF16)
    return pl.pallas_call(
        collect_kernel,
        in_specs=[SMEM] + [VMEM] * 12,
        out_specs=[VMEM] * 3,
        out_shape=[jax.ShapeDtypeStruct((ROWS, 1024), BF16), half, half],
        compiler_params=params(24),
        cost_estimate=cost(2 * ROWS * 1024 * 256, 0, 8 * ROWS * 1024),
        name="collect",
    )(place, *arrays)


def project(place, left, weights):
    return pl.pallas_call(
        project_kernel,
        in_specs=[SMEM, VMEM, VMEM],
        out_specs=[VMEM] * 3,
        out_shape=[jax.ShapeDtypeStruct((ROWS, 256), F32)] * 3,
        compiler_params=params(24),
        cost_estimate=cost(2 * ROWS * 1024 * 768, 0, 8 * ROWS * 1024),
        name="project",
    )(place, left, weights)


def compute(queries, key_rows, value_rows, attn_out, gate_pre, out_grad, segments, projections):
    core = lax.axis_index("seq") % 2
    head = lax.axis_index("head")
    front = core == 0
    core_at = core.reshape(1).astype(jnp.int32)

    def in_order(kept, received):
        return jnp.where(front, kept, received), jnp.where(front, received, kept)

    def halves(block):
        return in_order(block[:ROWS], block[ROWS:])

    def give(same, cross, target):
        same = move(same, target)
        cross = move(cross, lambda i: target(i) ^ 1)
        return same, cross

    def by_head(block):
        return in_order(block[:, :HEAD_DIM], block[:, HEAD_DIM:])

    users = (segments + 1).astype(BF16)
    users_recv = swap(users)
    kv_keep, kv_send = (
        jnp.concatenate(pair, axis=1) for pair in zip(by_head(key_rows), by_head(value_rows))
    )
    kv_recv = swap(kv_send)
    keep, send, gate_grad = by_rows(
        prepare_kernel, 3, core_at, queries, attn_out, gate_pre, out_grad
    )
    recv = swap(send)
    seg = jnp.concatenate(in_order(users, users_recv)).reshape(PAIR // 256, 256)
    seg = jnp.pad(seg, ((0, SEG_ROWS - PAIR // 256), (0, 0)))
    key = jnp.concatenate([*in_order(kv_keep, kv_recv), seg])
    odd = lambda i: i % 2 == 1
    key_prev = move(key, lambda i: -1 if odd(i) else i + 2)
    recv, key, seg = lax.optimization_barrier((recv, key, seg))
    low_rows, high_rows = in_order(keep, recv)
    next_a = shift(jnp.concatenate([low_rows, seg]), -2)
    next_b = shift(high_rows, -2)
    query = jnp.concatenate([low_rows, high_rows, seg])
    query_far = shift(query, -6)
    every, early, late = (0, 1, 2, 3), (0, 1), (2, 3)
    area = PAIR * PAIR
    dq0, dkv0 = pairs("pairs_own", [query], [WHOLE], key, F32, every, area // 2)
    next_a, dq0 = lax.optimization_barrier((next_a, dq0))
    dq1a, dkv1a = pairs("pairs_one", [next_a], [EARLY], key, BF16, early, area // 2)
    next_a, next_b, dq1a = lax.optimization_barrier((next_a, next_b, dq1a))
    query_next = jnp.concatenate([next_a[:ROWS], next_b, next_a[ROWS:]])
    query_two = move(query_next, lambda i: i - 2 if odd(i) else -1)
    dq1b, dkv1b = pairs("pairs_one", [query_next], [WHOLE], key, BF16, late, area // 2)
    back_same, back_cross = give(*in_order(dq1a, dq1b), lambda i: i + 2)
    query_far, dq1b = lax.optimization_barrier((query_far, dq1b))
    dq3, dkv3 = pairs("pairs_three", [query_far], [WHOLE], key, BF16, every, area // 8)
    far_same, far_cross = give(*halves(dq3), lambda i: i + 6)
    query_two, key_prev, dkv3 = lax.optimization_barrier((query_two, key_prev, dkv3))
    dq2, dkv2 = pairs(
        "pairs_two",
        [jnp.where(front, query_next, query_two)],
        [WHOLE],
        jnp.where(front, key_prev, key),
        BF16,
        every,
        area // 2,
    )
    key_same, key_cross = give(*halves(dkv2), lambda i: -9 if odd(i) else i - 2)
    two_same, two_cross = give(*halves(dq2), lambda i: i + 4 if odd(i) else i + 2)
    dkv = total(dkv0, dkv1a, dkv1b, dkv3, jnp.where(front, jnp.zeros_like(dkv2), dkv2))
    mine, other = halves(jnp.concatenate([dq0, dkv], axis=1))
    other = swap(other.astype(BF16))
    place = jnp.stack([core, head]).astype(jnp.int32)
    left, low, high = collect(
        place, mine, other, back_same, back_cross, far_same, far_cross, two_same, two_cross,
        key_same, key_cross, gate_grad, projections,
    )

    def turn(block, by):
        return lax.ppermute(block, "head", [(i, (i + by) % 4) for i in range(4)])

    low, high = turn(low, 1), turn(high, -1)
    after, before, result = project(place, left, projections)
    half = ROWS // 2
    after = jnp.concatenate([after[:half] + low.astype(F32), after[half:]]).astype(BF16)
    before = jnp.concatenate([before[:half], before[half:] + high.astype(F32)]).astype(BF16)
    return total(result, turn(after, 1), turn(before, -1)).astype(BF16)


def solution(mesh):
    split = P("seq", "head")
    return jax.shard_map(
        compute,
        mesh=mesh,
        in_specs=(split,) * 6 + (P("seq"), P(None, None, "head")),
        out_specs=split,
        check_vma=False,
    )
```

```python
import jax
import jax.numpy as jnp
from jax import lax
from jax.experimental import pallas as pl
from jax.experimental.pallas import tpu as pltpu
from jax.sharding import PartitionSpec as P


HEAD_DIM = 128
ROWS = 1024
PAIR = 2 * ROWS
SEG_ROWS = 16
TILE = 512
TILES = PAIR // TILE
HALF_SCALE = 0.5 * HEAD_DIM ** (-0.5)
VMEM = pl.BlockSpec(memory_space=pltpu.VMEM)
SMEM = pl.BlockSpec(memory_space=pltpu.SMEM)
BF16, F32 = jnp.bfloat16, jnp.float32


def cost(flops, transcendentals, size):
    return pl.CostEstimate(flops=flops, transcendentals=transcendentals, bytes_accessed=size)


def params(mib):
    return pltpu.CompilerParams(vmem_limit_bytes=mib * 2**20)


def move(block, target):
    devices = range(lax.axis_size("seq"))
    route = [(i, target(i)) for i in devices if target(i) in devices]
    return lax.ppermute(block, "seq", route)


def shift(block, distance):
    return move(block, lambda i: i + distance)


def swap(block):
    return lax.ppermute(block, "seq", [(i, i ^ 1) for i in range(lax.axis_size("seq"))])


def total(*terms):
    return sum(t.astype(F32) for t in terms)


def silu_slope(v):
    sigma = jax.nn.sigmoid(v)
    return sigma * (1.0 + v * (1.0 - sigma))


def prepare_kernel(core, q, o, gate, grad, keep, send, gate_grad):
    for slot, out in ((0, keep), (1, send)):
        head = core[0] if slot == 0 else 1 - core[0]
        cols = pl.ds(pl.multiple_of(head * HEAD_DIM, HEAD_DIM), HEAD_DIM)
        saved = o[:, cols].astype(F32)
        centred = saved - jnp.mean(saved, axis=-1, keepdims=True)
        inverse = lax.rsqrt(jnp.mean(centred * centred, axis=-1, keepdims=True) + 1e-06)
        normed = centred * inverse
        gate_in = gate[:, cols].astype(F32)
        grad_in = grad[:, cols].astype(F32)
        gate_grad[:, cols] = (grad_in * normed * silu_slope(gate_in)).astype(BF16)
        g = grad_in * jax.nn.silu(gate_in)
        attn_grad = inverse * (
            g
            - jnp.mean(g, axis=-1, keepdims=True)
            - normed * jnp.mean(g * normed, axis=-1, keepdims=True)
        )
        out[:, 0:128] = q[:, cols]
        out[:, 128:256] = attn_grad.astype(BF16)


def by_rows(kernel, outputs, core, *arrays):
    rows = 256
    wide = pl.BlockSpec((rows, 2 * HEAD_DIM), lambda i, c: (i, 0))
    return pl.pallas_call(
        kernel,
        grid_spec=pltpu.PrefetchScalarGridSpec(
            num_scalar_prefetch=1,
            grid=(ROWS // rows,),
            in_specs=[wide] * len(arrays),
            out_specs=[wide] * outputs,
        ),
        out_shape=[jax.ShapeDtypeStruct((ROWS, 2 * HEAD_DIM), BF16)] * outputs,
        compiler_params=params(60),
        cost_estimate=cost(30 * ROWS * 256, 2 * ROWS * 256, 8 * ROWS * 512),
    )(core, *arrays)


def pairs_kernel(own, parts, tiles, *refs):
    core, q_in, k_in = refs[0], refs[1:1 + len(parts)], refs[1 + len(parts)]
    *outs, q, k, dq, dk, dv, row_q, col_k, bound, todo, w0, d0, w1, d1, sem = refs[2 + len(parts):]
    copies = [pltpu.make_async_copy(k_in, k, sem.at[0])]
    for ref, moves in zip(q_in, parts):
        for source, target, size in moves:
            copies.append(
                pltpu.make_async_copy(
                    ref.at[pl.ds(source, size)], q.at[pl.ds(target, size)], sem.at[len(copies)]
                )
            )
    for copy in copies:
        copy.start()
    dq[...] = jnp.zeros_like(dq)
    dk[...] = jnp.zeros_like(dk)
    dv[...] = jnp.zeros_like(dv)
    for copy in copies:
        copy.wait()
    blocks = PAIR // 256
    users_q, users_k = q[PAIR:].astype(F32), k[PAIR:].astype(F32)
    padded = jnp.concatenate([users_k, jnp.zeros((128 - SEG_ROWS, 256), F32)])
    for half in range(2):
        turned = jnp.transpose(padded[:, half * 128:half * 128 + 128])
        for r in range(blocks):
            start = r * 256 + half * 128
            col_k[start:start + 128] = jnp.broadcast_to(turned[:, r:r + 1], (128, 128))
    for r in range(blocks):
        row_q[:, r * 256:(r + 1) * 256] = users_q[r:r + 1]
    row_q[:, PAIR:] = jnp.full((1, TILE), -1.0, F32)
    for b in range(TILES):
        rows = slice(b * TILE // 256, (b + 1) * TILE // 256)
        bound[0, b] = jnp.min(users_q[rows])
        bound[1, b] = jnp.max(users_q[rows])
        bound[2, b] = jnp.min(users_k[rows])
        bound[3, b] = jnp.max(users_k[rows])

    count = jnp.int32(0)
    for kt in range(TILES):
        for qt in tiles:
            if own and qt < kt:
                continue
            some = (bound[0, qt] <= bound[3, kt]) & (bound[1, qt] >= bound[2, kt])
            todo[0, count] = qt
            todo[1, count] = kt
            todo[2, count] = qt
            count = count + some.astype(jnp.int32)
    for extra in range(3):
        todo[0, count + extra] = tiles[0]
        todo[1, count + extra] = 0
        todo[2, count + extra] = TILES
    last = (((1,), (1,)), ((), ()))
    first = (((0,), (0,)), ((), ()))

    def rows_of(tile):
        return pl.ds(pl.multiple_of(tile * TILE, TILE), TILE)

    def score(n, w_out, d_out):
        qt, kt = todo[0, n], todo[1, n]
        q_at, k_at = rows_of(qt), rows_of(kt)
        s = lax.dot_general(k[k_at, 0:128], q[q_at, 0:128], last, preferred_element_type=F32)
        p = lax.dot_general(k[k_at, 128:256], q[q_at, 128:256], last, preferred_element_type=F32)
        allowed = col_k[k_at, 0:1] == row_q[:, rows_of(todo[2, n])]
        if own:
            ahead = (qt - kt) * TILE
            allowed = allowed & (
                lax.broadcasted_iota(jnp.int32, (TILE, TILE), 1) + ahead
                >= lax.broadcasted_iota(jnp.int32, (TILE, TILE), 0)
            )
        y = jnp.where(allowed, s * HALF_SCALE, -64.0)
        t = jnp.tanh(y)
        u = 1.0 + t
        w = y * u
        d_out[...] = (p * (u + w * (1.0 - t))).astype(BF16)
        w_out[...] = w.astype(BF16)

    def gather(n, w_in, d_in):
        q_at, k_at = rows_of(todo[0, n]), rows_of(todo[1, n])
        dv[k_at, :] += jnp.dot(w_in[...], q[q_at, 128:256], preferred_element_type=F32)
        dk[k_at, :] += jnp.dot(d_in[...], q[q_at, 0:128], preferred_element_type=F32)
        dq[q_at, :] += lax.dot_general(d_in[...], k[k_at, 0:128], first, preferred_element_type=F32)

    @pl.when(count > 0)
    def _():
        score(0, w0, d0)

        def two(j, carry):
            n = 2 * j
            score(n + 1, w1, d1)
            gather(n, w0, d0)
            score(n + 2, w0, d0)
            gather(n + 1, w1, d1)
            return carry

        lax.fori_loop(0, (count + 1) // 2, two, 0)

    for out, half in zip(outs[-2:], (core[0], 1 - core[0])):
        at = pl.ds(pl.multiple_of(half * ROWS, ROWS), ROWS)
        out[:, 0:128] = (dk[at, :] * HALF_SCALE).astype(out.dtype)
        out[:, 128:256] = dv[at, :].astype(out.dtype)
    if len(tiles) == TILES:
        for out, half in zip(outs[:2], (core[0], 1 - core[0])):
            at = pl.ds(pl.multiple_of(half * ROWS, ROWS), ROWS)
            out[...] = (dq[at, :] * HALF_SCALE).astype(out.dtype)
    else:
        out, at = outs[0], slice(tiles[0] * TILE, (tiles[-1] + 1) * TILE)
        out[...] = (dq[at] * HALF_SCALE).astype(out.dtype)


WHOLE = [(0, 0, PAIR + SEG_ROWS)]
EARLY = [(0, 0, ROWS), (ROWS, PAIR, SEG_ROWS)]
USERS_ONLY = [(ROWS, PAIR, SEG_ROWS)]
LATE = [(0, ROWS, ROWS)]


def pairs(name, core, queries, parts, key, kind, tiles, area):
    anywhere = pl.BlockSpec(memory_space=pl.ANY)
    return pl.pallas_call(
        lambda *refs: pairs_kernel(name == "pairs_own", parts, tiles, *refs),
        in_specs=[SMEM] + [anywhere] * (len(queries) + 1),
        out_specs=[VMEM] * (len(tiles) * TILE // ROWS + 2),
        out_shape=[jax.ShapeDtypeStruct((ROWS, 128), kind)] * (len(tiles) * TILE // ROWS)
        + [jax.ShapeDtypeStruct((ROWS, 256), kind)] * 2,
        scratch_shapes=[
            pltpu.VMEM((PAIR + SEG_ROWS, 256), BF16),
            pltpu.VMEM((PAIR + SEG_ROWS, 256), BF16),
            pltpu.VMEM((PAIR, 128), F32),
            pltpu.VMEM((PAIR, 128), F32),
            pltpu.VMEM((PAIR, 128), F32),
            pltpu.VMEM((1, PAIR + TILE), F32),
            pltpu.VMEM((PAIR, 128), F32),
            pltpu.SMEM((4, TILES), F32),
            pltpu.SMEM((3, TILES * TILES + 4), jnp.int32),
            pltpu.VMEM((TILE, TILE), BF16),
            pltpu.VMEM((TILE, TILE), BF16),
            pltpu.VMEM((TILE, TILE), BF16),
            pltpu.VMEM((TILE, TILE), BF16),
            pltpu.SemaphoreType.DMA((4,)),
        ],
        compiler_params=params(28),
        cost_estimate=cost(20 * area * 128, area, 8 * PAIR * 256),
    )(core, *queries, key)


def collect_kernel(place, dq, dkv, other, back_same, back_cross, far_same, far_cross, key_same, key_cross,
                   gate_grad, weights,
                   left, low, high):
    core, x = place[0], place[1]
    front = core == 0
    for p in range(3):
        cols = slice(p * 128, (p + 1) * 128)
        b = other[:, cols].astype(F32)
        if p == 0:
            a = dq[...] + total(back_same[...], far_same[...])
            b = b + total(back_cross[...], far_cross[...])
        else:
            part = slice((p - 1) * 128, p * 128)
            a, b = dkv[:, part] + key_same[:, part].astype(F32), b + key_cross[:, part].astype(F32)
        a, b = a.astype(BF16), b.astype(BF16)
        left[:, p * 256:p * 256 + 128] = jnp.where(front, a, b)
        left[:, p * 256 + 128:p * 256 + 256] = jnp.where(front, b, a)
    left[:, 768:1024] = gate_grad[...]
    far = head_block(left, weights, lax.rem(x + 2, 4)).astype(BF16)
    low[...] = far[:ROWS // 2]
    high[...] = far[ROWS // 2:]


def head_block(left, weights, dest):
    ds = pl.ds(pl.multiple_of(dest * 256, 256), 256)
    acc = None
    for p in range(4):
        term = lax.dot_general(
            left[:, p * 256:p * 256 + 256], weights[p, ds, :], (((1,), (1,)), ((), ())),
            preferred_element_type=F32,
        )
        acc = term if acc is None else acc + term
    return acc


def project_kernel(place, left, weights, after, before, own):
    x = place[1]
    after[...] = head_block(left, weights, lax.rem(x + 1, 4))
    before[...] = head_block(left, weights, lax.rem(x + 3, 4))
    own[...] = head_block(left, weights, x)


def collect(place, *arrays):
    half = jax.ShapeDtypeStruct((ROWS // 2, 256), BF16)
    return pl.pallas_call(
        collect_kernel,
        in_specs=[SMEM] + [VMEM] * 11,
        out_specs=[VMEM] * 3,
        out_shape=[jax.ShapeDtypeStruct((ROWS, 1024), BF16), half, half],
        compiler_params=params(24),
        cost_estimate=cost(2 * ROWS * 1024 * 256, 0, 8 * ROWS * 1024),
        name="collect",
    )(place, *arrays)


def project(place, left, weights):
    return pl.pallas_call(
        project_kernel,
        in_specs=[SMEM, VMEM, VMEM],
        out_specs=[VMEM] * 3,
        out_shape=[jax.ShapeDtypeStruct((ROWS, 256), F32)] * 3,
        compiler_params=params(24),
        cost_estimate=cost(2 * ROWS * 1024 * 768, 0, 8 * ROWS * 1024),
        name="project",
    )(place, left, weights)


def compute(queries, key_rows, value_rows, attn_out, gate_pre, out_grad, segments, projections):
    core = lax.axis_index("seq") % 2
    head = lax.axis_index("head")
    front = core == 0
    core_at = core.reshape(1).astype(jnp.int32)

    def in_order(kept, received):
        return jnp.where(front, kept, received), jnp.where(front, received, kept)

    def give(same, cross, target):
        same = move(same, target)
        cross = move(cross, lambda i: target(i) ^ 1)
        return same, cross

    def by_head(block):
        return in_order(block[:, :HEAD_DIM], block[:, HEAD_DIM:])

    users = (segments + 1).astype(BF16)
    users_recv = swap(users)
    kv_keep, kv_send = (
        jnp.concatenate(pair, axis=1) for pair in zip(by_head(key_rows), by_head(value_rows))
    )
    kv_recv = swap(kv_send)
    keep, send, gate_grad = by_rows(
        prepare_kernel, 3, core_at, queries, attn_out, gate_pre, out_grad
    )
    recv = swap(send)
    seg = jnp.concatenate(in_order(users, users_recv)).reshape(PAIR // 256, 256)
    seg = jnp.pad(seg, ((0, SEG_ROWS - PAIR // 256), (0, 0)))
    key = jnp.concatenate([*in_order(kv_keep, kv_recv), seg])
    key_prev = shift(key, 2)
    recv, key, seg = lax.optimization_barrier((recv, key, seg))
    low_rows, high_rows = in_order(keep, recv)
    next_a = shift(jnp.concatenate([low_rows, seg]), -2)
    next_b = shift(high_rows, -2)
    query = jnp.concatenate([low_rows, high_rows, seg])
    every, early, late = (0, 1, 2, 3), (0, 1), (2, 3)
    area = PAIR * PAIR
    dq0, dq0_other, *dkv0 = pairs(
        "pairs_own", core_at, [query], [WHOLE], key, F32, every, area // 2
    )
    next_a, dq0 = lax.optimization_barrier((next_a, dq0))
    dq1a, *dkv1a = pairs("pairs_one", core_at, [next_a], [EARLY], key, BF16, early, area // 2)
    query, next_a, next_b, key_prev, dq1a = lax.optimization_barrier(
        (query, next_a, next_b, key_prev, dq1a)
    )
    query_far = shift(query, -6)
    dq2_same, dq2_cross, *dkv2 = pairs(
        "pairs_two", core_at, [next_a, next_b], [EARLY, LATE], key_prev, BF16, every, area // 2
    )
    key_same, key_cross = give(*dkv2, lambda i: i - 2)
    next_b, dq2_same = lax.optimization_barrier((next_b, dq2_same))
    dq1b, *dkv1b = pairs(
        "pairs_one", core_at, [next_a, next_b], [USERS_ONLY, LATE], key, BF16, late, area // 2
    )
    same, cross = in_order(dq1a, dq1b)
    same, cross = total(same, dq2_same).astype(BF16), total(cross, dq2_cross).astype(BF16)
    back_same, back_cross = give(same, cross, lambda i: i + 2)
    query_far, dq1b = lax.optimization_barrier((query_far, dq1b))
    dq3_same, dq3_cross, *dkv3 = pairs(
        "pairs_three", core_at, [query_far], [WHOLE], key, BF16, every, area // 8
    )
    far_same, far_cross = give(dq3_same, dq3_cross, lambda i: i + 6)
    mine, other = (total(*terms) for terms in zip(dkv0, dkv1a, dkv1b, dkv3))
    other = swap(jnp.concatenate([dq0_other, other], axis=1).astype(BF16))
    place = jnp.stack([core, head]).astype(jnp.int32)
    left, low, high = collect(
        place, dq0, mine, other, back_same, back_cross, far_same, far_cross, key_same, key_cross,
        gate_grad, projections,
    )

    def turn(block, by):
        return lax.ppermute(block, "head", [(i, (i + by) % 4) for i in range(4)])

    low, high = turn(low, 1), turn(high, -1)
    after, before, result = project(place, left, projections)
    half = ROWS // 2
    after = jnp.concatenate([after[:half] + low.astype(F32), after[half:]]).astype(BF16)
    before = jnp.concatenate([before[:half], before[half:] + high.astype(F32)]).astype(BF16)
    return total(result, turn(after, 1), turn(before, -1)).astype(BF16)


def solution(mesh):
    split = P("seq", "head")
    return jax.shard_map(
        compute,
        mesh=mesh,
        in_specs=(split,) * 6 + (P("seq"), P(None, None, "head")),
        out_specs=split,
        check_vma=False,
    )
```

```python
import jax
import jax.numpy as jnp
from jax import lax
from jax.experimental import pallas as pl
from jax.experimental.pallas import tpu as pltpu
from jax.sharding import PartitionSpec as P


HEAD_DIM = 128
ROWS = 1024
PAIR = 2 * ROWS
SEG_ROWS = 16
TILE = 512
TILES = PAIR // TILE
HALF_SCALE = 0.5 * HEAD_DIM ** (-0.5)
VMEM = pl.BlockSpec(memory_space=pltpu.VMEM)
SMEM = pl.BlockSpec(memory_space=pltpu.SMEM)
BF16, F32 = jnp.bfloat16, jnp.float32


def cost(flops, transcendentals, size):
    return pl.CostEstimate(flops=flops, transcendentals=transcendentals, bytes_accessed=size)


def params(mib):
    return pltpu.CompilerParams(vmem_limit_bytes=mib * 2**20)


def move(block, target):
    devices = range(lax.axis_size("seq"))
    route = [(i, target(i)) for i in devices if target(i) in devices]
    return lax.ppermute(block, "seq", route)


def shift(block, distance):
    return move(block, lambda i: i + distance)


def swap(block):
    return lax.ppermute(block, "seq", [(i, i ^ 1) for i in range(lax.axis_size("seq"))])


def total(*terms):
    return sum(t.astype(F32) for t in terms)


def silu_slope(v):
    sigma = jax.nn.sigmoid(v)
    return sigma * (1.0 + v * (1.0 - sigma))


def prepare_kernel(core, q, o, gate, grad, keep, send, gate_grad):
    for slot, out in ((0, keep), (1, send)):
        head = core[0] if slot == 0 else 1 - core[0]
        cols = pl.ds(pl.multiple_of(head * HEAD_DIM, HEAD_DIM), HEAD_DIM)
        saved = o[:, cols].astype(F32)
        centred = saved - jnp.mean(saved, axis=-1, keepdims=True)
        inverse = lax.rsqrt(jnp.mean(centred * centred, axis=-1, keepdims=True) + 1e-06)
        normed = centred * inverse
        gate_in = gate[:, cols].astype(F32)
        grad_in = grad[:, cols].astype(F32)
        gate_grad[:, cols] = (grad_in * normed * silu_slope(gate_in)).astype(BF16)
        g = grad_in * jax.nn.silu(gate_in)
        attn_grad = inverse * (
            g
            - jnp.mean(g, axis=-1, keepdims=True)
            - normed * jnp.mean(g * normed, axis=-1, keepdims=True)
        )
        out[:, 0:128] = q[:, cols]
        out[:, 128:256] = attn_grad.astype(BF16)


def by_rows(kernel, outputs, core, *arrays):
    rows = 256
    wide = pl.BlockSpec((rows, 2 * HEAD_DIM), lambda i, c: (i, 0))
    return pl.pallas_call(
        kernel,
        grid_spec=pltpu.PrefetchScalarGridSpec(
            num_scalar_prefetch=1,
            grid=(ROWS // rows,),
            in_specs=[wide] * len(arrays),
            out_specs=[wide] * outputs,
        ),
        out_shape=[jax.ShapeDtypeStruct((ROWS, 2 * HEAD_DIM), BF16)] * outputs,
        compiler_params=params(60),
        cost_estimate=cost(30 * ROWS * 256, 2 * ROWS * 256, 8 * ROWS * 512),
    )(core, *arrays)


def pairs_kernel(own, parts, tiles, *refs):
    core, q_in, k_in = refs[0], refs[1:1 + len(parts)], refs[1 + len(parts)]
    *outs, q, k, dq, dk, dv, row_q, col_k, bound, todo, w0, d0, w1, d1, sem = refs[2 + len(parts):]
    copies = [pltpu.make_async_copy(k_in, k, sem.at[0])]
    for ref, moves in zip(q_in, parts):
        for source, target, size in moves:
            copies.append(
                pltpu.make_async_copy(
                    ref.at[pl.ds(source, size)], q.at[pl.ds(target, size)], sem.at[len(copies)]
                )
            )
    for copy in copies:
        copy.start()
    dq[...] = jnp.zeros_like(dq)
    dk[...] = jnp.zeros_like(dk)
    dv[...] = jnp.zeros_like(dv)
    for copy in copies:
        copy.wait()
    blocks = PAIR // 256
    users_q, users_k = q[PAIR:].astype(F32), k[PAIR:].astype(F32)
    padded = jnp.concatenate([users_k, jnp.zeros((128 - SEG_ROWS, 256), F32)])
    for half in range(2):
        turned = jnp.transpose(padded[:, half * 128:half * 128 + 128])
        for r in range(blocks):
            start = r * 256 + half * 128
            col_k[start:start + 128] = jnp.broadcast_to(turned[:, r:r + 1], (128, 128))
    for r in range(blocks):
        row_q[:, r * 256:(r + 1) * 256] = users_q[r:r + 1]
    row_q[:, PAIR:] = jnp.full((1, TILE), -1.0, F32)
    for b in range(TILES):
        rows = slice(b * TILE // 256, (b + 1) * TILE // 256)
        bound[0, b] = jnp.min(users_q[rows])
        bound[1, b] = jnp.max(users_q[rows])
        bound[2, b] = jnp.min(users_k[rows])
        bound[3, b] = jnp.max(users_k[rows])

    count = jnp.int32(0)
    for kt in range(TILES):
        for qt in tiles:
            if own and qt < kt:
                continue
            some = (bound[0, qt] <= bound[3, kt]) & (bound[1, qt] >= bound[2, kt])
            todo[0, count] = qt
            todo[1, count] = kt
            todo[2, count] = qt
            count = count + some.astype(jnp.int32)
    for extra in range(3):
        todo[0, count + extra] = tiles[0]
        todo[1, count + extra] = 0
        todo[2, count + extra] = TILES
    last = (((1,), (1,)), ((), ()))
    first = (((0,), (0,)), ((), ()))

    def rows_of(tile):
        return pl.ds(pl.multiple_of(tile * TILE, TILE), TILE)

    def score(n, w_out, d_out):
        qt, kt = todo[0, n], todo[1, n]
        q_at, k_at = rows_of(qt), rows_of(kt)
        s = lax.dot_general(k[k_at, 0:128], q[q_at, 0:128], last, preferred_element_type=F32)
        p = lax.dot_general(k[k_at, 128:256], q[q_at, 128:256], last, preferred_element_type=F32)
        allowed = col_k[k_at, 0:1] == row_q[:, rows_of(todo[2, n])]
        if own:
            ahead = (qt - kt) * TILE
            allowed = allowed & (
                lax.broadcasted_iota(jnp.int32, (TILE, TILE), 1) + ahead
                >= lax.broadcasted_iota(jnp.int32, (TILE, TILE), 0)
            )
        y = jnp.where(allowed, s * HALF_SCALE, -64.0)
        t = jnp.tanh(y)
        u = 1.0 + t
        w = y * u
        d_out[...] = (p * (u + w * (1.0 - t))).astype(BF16)
        w_out[...] = w.astype(BF16)

    def gather(n, w_in, d_in):
        q_at, k_at = rows_of(todo[0, n]), rows_of(todo[1, n])
        dv[k_at, :] += jnp.dot(w_in[...], q[q_at, 128:256], preferred_element_type=F32)
        dk[k_at, :] += jnp.dot(d_in[...], q[q_at, 0:128], preferred_element_type=F32)
        dq[q_at, :] += lax.dot_general(d_in[...], k[k_at, 0:128], first, preferred_element_type=F32)

    @pl.when(count > 0)
    def _():
        score(0, w0, d0)

        def two(j, carry):
            n = 2 * j
            score(n + 1, w1, d1)
            gather(n, w0, d0)
            score(n + 2, w0, d0)
            gather(n + 1, w1, d1)
            return carry

        lax.fori_loop(0, (count + 1) // 2, two, 0)

    for out, half in zip(outs[-2:], (core[0], 1 - core[0])):
        at = pl.ds(pl.multiple_of(half * ROWS, ROWS), ROWS)
        out[:, 0:128] = (dk[at, :] * HALF_SCALE).astype(out.dtype)
        out[:, 128:256] = dv[at, :].astype(out.dtype)
    if len(tiles) == TILES:
        for out, half in zip(outs[:2], (core[0], 1 - core[0])):
            at = pl.ds(pl.multiple_of(half * ROWS, ROWS), ROWS)
            out[...] = (dq[at, :] * HALF_SCALE).astype(out.dtype)
    else:
        out, at = outs[0], slice(tiles[0] * TILE, (tiles[-1] + 1) * TILE)
        out[...] = (dq[at] * HALF_SCALE).astype(out.dtype)


WHOLE = [(0, 0, PAIR + SEG_ROWS)]
EARLY = [(0, 0, ROWS), (ROWS, PAIR, SEG_ROWS)]
USERS_ONLY = [(ROWS, PAIR, SEG_ROWS)]
LATE = [(0, ROWS, ROWS)]


def pairs(name, core, queries, parts, key, kind, tiles, area):
    anywhere = pl.BlockSpec(memory_space=pl.ANY)
    return pl.pallas_call(
        lambda *refs: pairs_kernel(name == "pairs_own", parts, tiles, *refs),
        in_specs=[SMEM] + [anywhere] * (len(queries) + 1),
        out_specs=[VMEM] * (len(tiles) * TILE // ROWS + 2),
        out_shape=[jax.ShapeDtypeStruct((ROWS, 128), kind)] * (len(tiles) * TILE // ROWS)
        + [jax.ShapeDtypeStruct((ROWS, 256), kind)] * 2,
        scratch_shapes=[
            pltpu.VMEM((PAIR + SEG_ROWS, 256), BF16),
            pltpu.VMEM((PAIR + SEG_ROWS, 256), BF16),
            pltpu.VMEM((PAIR, 128), F32),
            pltpu.VMEM((PAIR, 128), F32),
            pltpu.VMEM((PAIR, 128), F32),
            pltpu.VMEM((1, PAIR + TILE), F32),
            pltpu.VMEM((PAIR, 128), F32),
            pltpu.SMEM((4, TILES), F32),
            pltpu.SMEM((3, TILES * TILES + 4), jnp.int32),
            pltpu.VMEM((TILE, TILE), BF16),
            pltpu.VMEM((TILE, TILE), BF16),
            pltpu.VMEM((TILE, TILE), BF16),
            pltpu.VMEM((TILE, TILE), BF16),
            pltpu.SemaphoreType.DMA((4,)),
        ],
        compiler_params=params(28),
        cost_estimate=cost(20 * area * 128, area, 8 * PAIR * 256),
    )(core, *queries, key)


def collect_kernel(place, dq, dkv, other, back_same, back_cross, far_same, far_cross, key_same, key_cross,
                   gate_grad, weights,
                   left, low, high):
    core, x = place[0], place[1]
    front = core == 0
    for p in range(3):
        cols = slice(p * 128, (p + 1) * 128)
        b = other[:, cols].astype(F32)
        if p == 0:
            a = dq[...] + total(back_same[...], far_same[...])
            b = b + total(back_cross[...], far_cross[...])
        else:
            part = slice((p - 1) * 128, p * 128)
            a, b = dkv[:, part] + key_same[:, part].astype(F32), b + key_cross[:, part].astype(F32)
        a, b = a.astype(BF16), b.astype(BF16)
        left[:, p * 256:p * 256 + 128] = jnp.where(front, a, b)
        left[:, p * 256 + 128:p * 256 + 256] = jnp.where(front, b, a)
    left[:, 768:1024] = gate_grad[...]
    far = head_block(left, weights, lax.rem(x + 2, 4)).astype(BF16)
    low[...] = far[:ROWS // 2]
    high[...] = far[ROWS // 2:]


def head_block(left, weights, dest):
    ds = pl.ds(pl.multiple_of(dest * 256, 256), 256)
    acc = None
    for p in range(4):
        term = lax.dot_general(
            left[:, p * 256:p * 256 + 256], weights[p, ds, :], (((1,), (1,)), ((), ())),
            preferred_element_type=F32,
        )
        acc = term if acc is None else acc + term
    return acc


def project_kernel(place, left, weights, after, before, own):
    x = place[1]
    after[...] = head_block(left, weights, lax.rem(x + 1, 4))
    before[...] = head_block(left, weights, lax.rem(x + 3, 4))
    own[...] = head_block(left, weights, x)


def collect(place, *arrays):
    half = jax.ShapeDtypeStruct((ROWS // 2, 256), BF16)
    return pl.pallas_call(
        collect_kernel,
        in_specs=[SMEM] + [VMEM] * 11,
        out_specs=[VMEM] * 3,
        out_shape=[jax.ShapeDtypeStruct((ROWS, 1024), BF16), half, half],
        compiler_params=params(24),
        cost_estimate=cost(2 * ROWS * 1024 * 256, 0, 8 * ROWS * 1024),
        name="collect",
    )(place, *arrays)


def project(place, left, weights):
    return pl.pallas_call(
        project_kernel,
        in_specs=[SMEM, VMEM, VMEM],
        out_specs=[VMEM] * 3,
        out_shape=[jax.ShapeDtypeStruct((ROWS, 256), F32)] * 3,
        compiler_params=params(24),
        cost_estimate=cost(2 * ROWS * 1024 * 768, 0, 8 * ROWS * 1024),
        name="project",
    )(place, left, weights)


def compute(queries, key_rows, value_rows, attn_out, gate_pre, out_grad, segments, projections):
    core = lax.axis_index("seq") % 2
    head = lax.axis_index("head")
    front = core == 0
    core_at = core.reshape(1).astype(jnp.int32)

    def in_order(kept, received):
        return jnp.where(front, kept, received), jnp.where(front, received, kept)

    def give(same, cross, target):
        same = move(same, target)
        cross = move(cross, lambda i: target(i) ^ 1)
        return same, cross

    def by_head(block):
        return in_order(block[:, :HEAD_DIM], block[:, HEAD_DIM:])

    users = (segments + 1).astype(BF16)
    users_recv = swap(users)
    kv_keep, kv_send = (
        jnp.concatenate(pair, axis=1) for pair in zip(by_head(key_rows), by_head(value_rows))
    )
    kv_recv = swap(kv_send)
    keep, send, gate_grad = by_rows(
        prepare_kernel, 3, core_at, queries, attn_out, gate_pre, out_grad
    )
    recv = swap(send)
    seg = jnp.concatenate(in_order(users, users_recv)).reshape(PAIR // 256, 256)
    seg = jnp.pad(seg, ((0, SEG_ROWS - PAIR // 256), (0, 0)))
    key = jnp.concatenate([*in_order(kv_keep, kv_recv), seg])
    key_prev = shift(key, 2)
    recv, key, seg = lax.optimization_barrier((recv, key, seg))
    low_rows, high_rows = in_order(keep, recv)
    next_a = shift(jnp.concatenate([low_rows, seg]), -2)
    next_b = shift(high_rows, -2)
    query = jnp.concatenate([low_rows, high_rows, seg])
    every, early, late = (0, 1, 2, 3), (0, 1), (2, 3)
    area = PAIR * PAIR
    dq0, dq0_other, *dkv0 = pairs(
        "pairs_own", core_at, [query], [WHOLE], key, F32, every, area // 2
    )
    query, next_a, dq0 = lax.optimization_barrier((query, next_a, dq0))
    query_far = shift(query, -6)
    dq1a, *dkv1a = pairs("pairs_one", core_at, [next_a], [EARLY], key, BF16, early, area // 2)
    next_a, next_b, key_prev, dq1a = lax.optimization_barrier((next_a, next_b, key_prev, dq1a))
    dq2_same, dq2_cross, *dkv2 = pairs(
        "pairs_two", core_at, [next_a, next_b], [EARLY, LATE], key_prev, BF16, every, area // 2
    )
    key_same, key_cross = give(*dkv2, lambda i: i - 2)
    query_far, dq2_same = lax.optimization_barrier((query_far, dq2_same))
    dq3_same, dq3_cross, *dkv3 = pairs(
        "pairs_three", core_at, [query_far], [WHOLE], key, BF16, every, area // 8
    )
    far_same, far_cross = give(dq3_same, dq3_cross, lambda i: i + 6)
    next_b, dq3_same = lax.optimization_barrier((next_b, dq3_same))
    dq1b, *dkv1b = pairs(
        "pairs_one", core_at, [next_a, next_b], [USERS_ONLY, LATE], key, BF16, late, area // 2
    )
    same, cross = in_order(dq1a, dq1b)
    same, cross = total(same, dq2_same).astype(BF16), total(cross, dq2_cross).astype(BF16)
    back_same, back_cross = give(same, cross, lambda i: i + 2)
    mine, other = (total(*terms) for terms in zip(dkv0, dkv1a, dkv1b, dkv3))
    other = swap(jnp.concatenate([dq0_other, other], axis=1).astype(BF16))
    place = jnp.stack([core, head]).astype(jnp.int32)
    left, low, high = collect(
        place, dq0, mine, other, back_same, back_cross, far_same, far_cross, key_same, key_cross,
        gate_grad, projections,
    )

    def turn(block, by):
        return lax.ppermute(block, "head", [(i, (i + by) % 4) for i in range(4)])

    low, high = turn(low, 1), turn(high, -1)
    after, before, result = project(place, left, projections)
    half = ROWS // 2
    after = jnp.concatenate([after[:half] + low.astype(F32), after[half:]]).astype(BF16)
    before = jnp.concatenate([before[:half], before[half:] + high.astype(F32)]).astype(BF16)
    return total(result, turn(after, 1), turn(before, -1)).astype(BF16)


def solution(mesh):
    split = P("seq", "head")
    return jax.shard_map(
        compute,
        mesh=mesh,
        in_specs=(split,) * 6 + (P("seq"), P(None, None, "head")),
        out_specs=split,
        check_vma=False,
    )
```

```python
import jax
import jax.numpy as jnp
from jax import lax
from jax.experimental import pallas as pl
from jax.experimental.pallas import tpu as pltpu
from jax.sharding import PartitionSpec as P


HEAD_DIM = 128
ROWS = 1024
PAIR = 2 * ROWS
SEG_ROWS = 16
TILE = 512
TILES = PAIR // TILE
HALF_SCALE = 0.5 * HEAD_DIM ** (-0.5)
VMEM = pl.BlockSpec(memory_space=pltpu.VMEM)
SMEM = pl.BlockSpec(memory_space=pltpu.SMEM)
BF16, F32 = jnp.bfloat16, jnp.float32


def cost(flops, transcendentals, size):
    return pl.CostEstimate(flops=flops, transcendentals=transcendentals, bytes_accessed=size)


def params(mib):
    return pltpu.CompilerParams(vmem_limit_bytes=mib * 2**20)


def move(block, target):
    devices = range(lax.axis_size("seq"))
    route = [(i, target(i)) for i in devices if target(i) in devices]
    return lax.ppermute(block, "seq", route)


def shift(block, distance):
    return move(block, lambda i: i + distance)


def swap(block):
    return lax.ppermute(block, "seq", [(i, i ^ 1) for i in range(lax.axis_size("seq"))])


def total(*terms):
    return sum(t.astype(F32) for t in terms)


def silu_slope(v):
    sigma = jax.nn.sigmoid(v)
    return sigma * (1.0 + v * (1.0 - sigma))


def prepare_kernel(core, q, o, gate, grad, keep, send, gate_grad):
    for slot, out in ((0, keep), (1, send)):
        head = core[0] if slot == 0 else 1 - core[0]
        cols = pl.ds(pl.multiple_of(head * HEAD_DIM, HEAD_DIM), HEAD_DIM)
        saved = o[:, cols].astype(F32)
        centred = saved - jnp.mean(saved, axis=-1, keepdims=True)
        inverse = lax.rsqrt(jnp.mean(centred * centred, axis=-1, keepdims=True) + 1e-06)
        normed = centred * inverse
        gate_in = gate[:, cols].astype(F32)
        grad_in = grad[:, cols].astype(F32)
        gate_grad[:, cols] = (grad_in * normed * silu_slope(gate_in)).astype(BF16)
        g = grad_in * jax.nn.silu(gate_in)
        attn_grad = inverse * (
            g
            - jnp.mean(g, axis=-1, keepdims=True)
            - normed * jnp.mean(g * normed, axis=-1, keepdims=True)
        )
        out[:, 0:128] = q[:, cols]
        out[:, 128:256] = attn_grad.astype(BF16)


def by_rows(kernel, outputs, core, *arrays):
    rows = 512
    wide = pl.BlockSpec((rows, 2 * HEAD_DIM), lambda i, c: (i, 0))
    return pl.pallas_call(
        kernel,
        grid_spec=pltpu.PrefetchScalarGridSpec(
            num_scalar_prefetch=1,
            grid=(ROWS // rows,),
            in_specs=[wide] * len(arrays),
            out_specs=[wide] * outputs,
        ),
        out_shape=[jax.ShapeDtypeStruct((ROWS, 2 * HEAD_DIM), BF16)] * outputs,
        compiler_params=params(60),
        cost_estimate=cost(30 * ROWS * 256, 2 * ROWS * 256, 8 * ROWS * 512),
    )(core, *arrays)


def pairs_kernel(own, parts, tiles, *refs):
    core, q_in, k_in = refs[0], refs[1:1 + len(parts)], refs[1 + len(parts)]
    *outs, q, k, dq, dk, dv, row_q, col_k, bound, todo, w0, d0, w1, d1, sem = refs[2 + len(parts):]
    copies = [pltpu.make_async_copy(k_in, k, sem.at[0])]
    for ref, moves in zip(q_in, parts):
        for source, target, size in moves:
            copies.append(
                pltpu.make_async_copy(
                    ref.at[pl.ds(source, size)], q.at[pl.ds(target, size)], sem.at[len(copies)]
                )
            )
    for copy in copies:
        copy.start()
    dq[...] = jnp.zeros_like(dq)
    dk[...] = jnp.zeros_like(dk)
    dv[...] = jnp.zeros_like(dv)
    for copy in copies:
        copy.wait()
    blocks = PAIR // 256
    users_q, users_k = q[PAIR:].astype(F32), k[PAIR:].astype(F32)
    padded = jnp.concatenate([users_k, jnp.zeros((128 - SEG_ROWS, 256), F32)])
    for half in range(2):
        turned = jnp.transpose(padded[:, half * 128:half * 128 + 128])
        for r in range(blocks):
            start = r * 256 + half * 128
            col_k[start:start + 128] = jnp.broadcast_to(turned[:, r:r + 1], (128, 128))
    for r in range(blocks):
        row_q[:, r * 256:(r + 1) * 256] = users_q[r:r + 1]
    row_q[:, PAIR:] = jnp.full((1, TILE), -1.0, F32)
    for b in range(TILES):
        rows = slice(b * TILE // 256, (b + 1) * TILE // 256)
        bound[0, b] = jnp.min(users_q[rows])
        bound[1, b] = jnp.max(users_q[rows])
        bound[2, b] = jnp.min(users_k[rows])
        bound[3, b] = jnp.max(users_k[rows])

    count = jnp.int32(0)
    for kt in range(TILES):
        for qt in tiles:
            if own and qt < kt:
                continue
            some = (bound[0, qt] <= bound[3, kt]) & (bound[1, qt] >= bound[2, kt])
            todo[0, count] = qt
            todo[1, count] = kt
            todo[2, count] = qt
            count = count + some.astype(jnp.int32)
    for extra in range(3):
        todo[0, count + extra] = tiles[0]
        todo[1, count + extra] = 0
        todo[2, count + extra] = TILES
    last = (((1,), (1,)), ((), ()))
    first = (((0,), (0,)), ((), ()))

    def rows_of(tile):
        return pl.ds(pl.multiple_of(tile * TILE, TILE), TILE)

    def score(n, w_out, d_out):
        qt, kt = todo[0, n], todo[1, n]
        q_at, k_at = rows_of(qt), rows_of(kt)
        s = lax.dot_general(k[k_at, 0:128], q[q_at, 0:128], last, preferred_element_type=F32)
        p = lax.dot_general(k[k_at, 128:256], q[q_at, 128:256], last, preferred_element_type=F32)
        allowed = col_k[k_at, 0:1] == row_q[:, rows_of(todo[2, n])]
        if own:
            ahead = (qt - kt) * TILE
            allowed = allowed & (
                lax.broadcasted_iota(jnp.int32, (TILE, TILE), 1) + ahead
                >= lax.broadcasted_iota(jnp.int32, (TILE, TILE), 0)
            )
        y = jnp.where(allowed, s * HALF_SCALE, -64.0)
        t = jnp.tanh(y)
        u = 1.0 + t
        w = y * u
        d_out[...] = (p * (u + w * (1.0 - t))).astype(BF16)
        w_out[...] = w.astype(BF16)

    def gather(n, w_in, d_in):
        q_at, k_at = rows_of(todo[0, n]), rows_of(todo[1, n])
        dv[k_at, :] += jnp.dot(w_in[...], q[q_at, 128:256], preferred_element_type=F32)
        dk[k_at, :] += jnp.dot(d_in[...], q[q_at, 0:128], preferred_element_type=F32)
        dq[q_at, :] += lax.dot_general(d_in[...], k[k_at, 0:128], first, preferred_element_type=F32)

    @pl.when(count > 0)
    def _():
        score(0, w0, d0)

        def two(j, carry):
            n = 2 * j
            score(n + 1, w1, d1)
            gather(n, w0, d0)
            score(n + 2, w0, d0)
            gather(n + 1, w1, d1)
            return carry

        lax.fori_loop(0, (count + 1) // 2, two, 0)

    for out, half in zip(outs[-2:], (core[0], 1 - core[0])):
        at = pl.ds(pl.multiple_of(half * ROWS, ROWS), ROWS)
        out[:, 0:128] = (dk[at, :] * HALF_SCALE).astype(out.dtype)
        out[:, 128:256] = dv[at, :].astype(out.dtype)
    if len(tiles) == TILES:
        for out, half in zip(outs[:2], (core[0], 1 - core[0])):
            at = pl.ds(pl.multiple_of(half * ROWS, ROWS), ROWS)
            out[...] = (dq[at, :] * HALF_SCALE).astype(out.dtype)
    else:
        out, at = outs[0], slice(tiles[0] * TILE, (tiles[-1] + 1) * TILE)
        out[...] = (dq[at] * HALF_SCALE).astype(out.dtype)


WHOLE = [(0, 0, PAIR + SEG_ROWS)]
EARLY = [(0, 0, ROWS), (ROWS, PAIR, SEG_ROWS)]
USERS_ONLY = [(ROWS, PAIR, SEG_ROWS)]
LATE = [(0, ROWS, ROWS)]


def pairs(name, core, queries, parts, key, kind, tiles, area):
    anywhere = pl.BlockSpec(memory_space=pl.ANY)
    return pl.pallas_call(
        lambda *refs: pairs_kernel(name == "pairs_own", parts, tiles, *refs),
        in_specs=[SMEM] + [anywhere] * (len(queries) + 1),
        out_specs=[VMEM] * (len(tiles) * TILE // ROWS + 2),
        out_shape=[jax.ShapeDtypeStruct((ROWS, 128), kind)] * (len(tiles) * TILE // ROWS)
        + [jax.ShapeDtypeStruct((ROWS, 256), kind)] * 2,
        scratch_shapes=[
            pltpu.VMEM((PAIR + SEG_ROWS, 256), BF16),
            pltpu.VMEM((PAIR + SEG_ROWS, 256), BF16),
            pltpu.VMEM((PAIR, 128), F32),
            pltpu.VMEM((PAIR, 128), F32),
            pltpu.VMEM((PAIR, 128), F32),
            pltpu.VMEM((1, PAIR + TILE), F32),
            pltpu.VMEM((PAIR, 128), F32),
            pltpu.SMEM((4, TILES), F32),
            pltpu.SMEM((3, TILES * TILES + 4), jnp.int32),
            pltpu.VMEM((TILE, TILE), BF16),
            pltpu.VMEM((TILE, TILE), BF16),
            pltpu.VMEM((TILE, TILE), BF16),
            pltpu.VMEM((TILE, TILE), BF16),
            pltpu.SemaphoreType.DMA((4,)),
        ],
        compiler_params=params(28),
        cost_estimate=cost(20 * area * 128, area, 8 * PAIR * 256),
    )(core, *queries, key)


def collect_kernel(place, dq, dkv, other, back_same, back_cross, far_same, far_cross, key_same, key_cross,
                   gate_grad, weights,
                   left, low, high):
    core, x = place[0], place[1]
    front = core == 0
    for p in range(3):
        cols = slice(p * 128, (p + 1) * 128)
        b = other[:, cols].astype(F32)
        if p == 0:
            a = dq[...] + total(back_same[...], far_same[...])
            b = b + total(back_cross[...], far_cross[...])
        else:
            part = slice((p - 1) * 128, p * 128)
            a, b = dkv[:, part] + key_same[:, part].astype(F32), b + key_cross[:, part].astype(F32)
        a, b = a.astype(BF16), b.astype(BF16)
        left[:, p * 256:p * 256 + 128] = jnp.where(front, a, b)
        left[:, p * 256 + 128:p * 256 + 256] = jnp.where(front, b, a)
    left[:, 768:1024] = gate_grad[...]
    far = head_block(left, weights, lax.rem(x + 2, 4)).astype(BF16)
    low[...] = far[:ROWS // 2]
    high[...] = far[ROWS // 2:]


def head_block(left, weights, dest):
    ds = pl.ds(pl.multiple_of(dest * 256, 256), 256)
    acc = None
    for p in range(4):
        term = lax.dot_general(
            left[:, p * 256:p * 256 + 256], weights[p, ds, :], (((1,), (1,)), ((), ())),
            preferred_element_type=F32,
        )
        acc = term if acc is None else acc + term
    return acc


def project_kernel(place, left, weights, after, before, own):
    x = place[1]
    after[...] = head_block(left, weights, lax.rem(x + 1, 4))
    before[...] = head_block(left, weights, lax.rem(x + 3, 4))
    own[...] = head_block(left, weights, x)


def collect(place, *arrays):
    half = jax.ShapeDtypeStruct((ROWS // 2, 256), BF16)
    return pl.pallas_call(
        collect_kernel,
        in_specs=[SMEM] + [VMEM] * 11,
        out_specs=[VMEM] * 3,
        out_shape=[jax.ShapeDtypeStruct((ROWS, 1024), BF16), half, half],
        compiler_params=params(24),
        cost_estimate=cost(2 * ROWS * 1024 * 256, 0, 8 * ROWS * 1024),
        name="collect",
    )(place, *arrays)


def project(place, left, weights):
    return pl.pallas_call(
        project_kernel,
        in_specs=[SMEM, VMEM, VMEM],
        out_specs=[VMEM] * 3,
        out_shape=[jax.ShapeDtypeStruct((ROWS, 256), F32)] * 3,
        compiler_params=params(24),
        cost_estimate=cost(2 * ROWS * 1024 * 768, 0, 8 * ROWS * 1024),
        name="project",
    )(place, left, weights)


def compute(queries, key_rows, value_rows, attn_out, gate_pre, out_grad, segments, projections):
    core = lax.axis_index("seq") % 2
    head = lax.axis_index("head")
    front = core == 0
    core_at = core.reshape(1).astype(jnp.int32)

    def in_order(kept, received):
        return jnp.where(front, kept, received), jnp.where(front, received, kept)

    def give(same, cross, target):
        same = move(same, target)
        cross = move(cross, lambda i: target(i) ^ 1)
        return same, cross

    def by_head(block):
        return in_order(block[:, :HEAD_DIM], block[:, HEAD_DIM:])

    users = (segments + 1).astype(BF16)
    users_recv = swap(users)
    kv_keep, kv_send = (
        jnp.concatenate(pair, axis=1) for pair in zip(by_head(key_rows), by_head(value_rows))
    )
    kv_recv = swap(kv_send)
    keep, send, gate_grad = by_rows(
        prepare_kernel, 3, core_at, queries, attn_out, gate_pre, out_grad
    )
    recv = swap(send)
    seg = jnp.concatenate(in_order(users, users_recv)).reshape(PAIR // 256, 256)
    seg = jnp.pad(seg, ((0, SEG_ROWS - PAIR // 256), (0, 0)))
    key = jnp.concatenate([*in_order(kv_keep, kv_recv), seg])
    key_prev = shift(key, 2)
    recv, key, seg = lax.optimization_barrier((recv, key, seg))
    low_rows, high_rows = in_order(keep, recv)
    next_a = shift(jnp.concatenate([low_rows, seg]), -2)
    next_b = shift(high_rows, -2)
    query = jnp.concatenate([low_rows, high_rows, seg])
    every, early, late = (0, 1, 2, 3), (0, 1), (2, 3)
    area = PAIR * PAIR
    dq0, dq0_other, *dkv0 = pairs(
        "pairs_own", core_at, [query], [WHOLE], key, F32, every, area // 2
    )
    next_a, dq0 = lax.optimization_barrier((next_a, dq0))
    dq1a, *dkv1a = pairs("pairs_one", core_at, [next_a], [EARLY], key, BF16, early, area // 2)
    query, next_a, next_b, key_prev, dq1a = lax.optimization_barrier(
        (query, next_a, next_b, key_prev, dq1a)
    )
    query_far = shift(query, -6)
    dq2_same, dq2_cross, *dkv2 = pairs(
        "pairs_two", core_at, [next_a, next_b], [EARLY, LATE], key_prev, BF16, every, area // 2
    )
    key_same, key_cross = give(*dkv2, lambda i: i - 2)
    next_b, dq2_same = lax.optimization_barrier((next_b, dq2_same))
    dq1b, *dkv1b = pairs(
        "pairs_one", core_at, [next_a, next_b], [USERS_ONLY, LATE], key, BF16, late, area // 2
    )
    query_far, dq1b = lax.optimization_barrier((query_far, dq1b))
    dq3_same, dq3_cross, *dkv3 = pairs(
        "pairs_three", core_at, [query_far], [WHOLE], key, BF16, every, area // 8
    )
    far_same, far_cross = give(dq3_same, dq3_cross, lambda i: i + 6)
    same, cross = in_order(dq1a, dq1b)
    same, cross = total(same, dq2_same).astype(BF16), total(cross, dq2_cross).astype(BF16)
    back_same, back_cross = give(same, cross, lambda i: i + 2)
    mine = total(dkv0[0], dkv1a[0], dkv1b[0], dkv3[0])
    other = total(dkv0[1], dkv1a[1], dkv1b[1], dkv3[1])
    other = jnp.concatenate([dq0_other, other], axis=1).astype(BF16)
    other = swap(other)
    place = jnp.stack([core, head]).astype(jnp.int32)
    left, low, high = collect(
        place, dq0, mine, other, back_same, back_cross, far_same, far_cross, key_same, key_cross,
        gate_grad, projections,
    )

    def turn(block, by):
        return lax.ppermute(block, "head", [(i, (i + by) % 4) for i in range(4)])

    low, high = turn(low, 1), turn(high, -1)
    after, before, result = project(place, left, projections)
    half = ROWS // 2
    after = jnp.concatenate([after[:half] + low.astype(F32), after[half:]]).astype(BF16)
    before = jnp.concatenate([before[:half], before[half:] + high.astype(F32)]).astype(BF16)
    return total(result, turn(after, 1), turn(before, -1)).astype(BF16)


def solution(mesh):
    split = P("seq", "head")
    return jax.shard_map(
        compute,
        mesh=mesh,
        in_specs=(split,) * 6 + (P("seq"), P(None, None, "head")),
        out_specs=split,
        check_vma=False,
    )
```

```python
import jax
import jax.numpy as jnp
from jax import lax
from jax.experimental import pallas as pl
from jax.experimental.pallas import tpu as pltpu
from jax.sharding import PartitionSpec as P


HEAD_DIM = 128
ROWS = 1024
PAIR = 2 * ROWS
SEG_ROWS = 16
TILE = 512
TILES = PAIR // TILE
HALF_SCALE = 0.5 * HEAD_DIM ** (-0.5)
VMEM = pl.BlockSpec(memory_space=pltpu.VMEM)
SMEM = pl.BlockSpec(memory_space=pltpu.SMEM)
BF16, F32 = jnp.bfloat16, jnp.float32


def cost(flops, transcendentals, size):
    return pl.CostEstimate(flops=flops, transcendentals=transcendentals, bytes_accessed=size)


def params(mib):
    return pltpu.CompilerParams(vmem_limit_bytes=mib * 2**20)


def move(block, target):
    devices = range(lax.axis_size("seq"))
    route = [(i, target(i)) for i in devices if target(i) in devices]
    return lax.ppermute(block, "seq", route)


def shift(block, distance):
    return move(block, lambda i: i + distance)


def swap(block):
    return lax.ppermute(block, "seq", [(i, i ^ 1) for i in range(lax.axis_size("seq"))])


def total(*terms):
    return sum(t.astype(F32) for t in terms)


def silu_slope(v):
    sigma = jax.nn.sigmoid(v)
    return sigma * (1.0 + v * (1.0 - sigma))


def prepare_kernel(core, q, o, gate, grad, keep, send, gate_grad):
    for slot, out in ((0, keep), (1, send)):
        head = core[0] if slot == 0 else 1 - core[0]
        cols = pl.ds(pl.multiple_of(head * HEAD_DIM, HEAD_DIM), HEAD_DIM)
        saved = o[:, cols].astype(F32)
        centred = saved - jnp.mean(saved, axis=-1, keepdims=True)
        inverse = lax.rsqrt(jnp.mean(centred * centred, axis=-1, keepdims=True) + 1e-06)
        normed = centred * inverse
        gate_in = gate[:, cols].astype(F32)
        grad_in = grad[:, cols].astype(F32)
        gate_grad[:, cols] = (grad_in * normed * silu_slope(gate_in)).astype(BF16)
        g = grad_in * jax.nn.silu(gate_in)
        attn_grad = inverse * (
            g
            - jnp.mean(g, axis=-1, keepdims=True)
            - normed * jnp.mean(g * normed, axis=-1, keepdims=True)
        )
        out[:, 0:128] = q[:, cols]
        out[:, 128:256] = attn_grad.astype(BF16)


def by_rows(kernel, outputs, core, *arrays):
    rows = 512
    wide = pl.BlockSpec((rows, 2 * HEAD_DIM), lambda i, c: (i, 0))
    return pl.pallas_call(
        kernel,
        grid_spec=pltpu.PrefetchScalarGridSpec(
            num_scalar_prefetch=1,
            grid=(ROWS // rows,),
            in_specs=[wide] * len(arrays),
            out_specs=[wide] * outputs,
        ),
        out_shape=[jax.ShapeDtypeStruct((ROWS, 2 * HEAD_DIM), BF16)] * outputs,
        compiler_params=params(60),
        cost_estimate=cost(30 * ROWS * 256, 2 * ROWS * 256, 8 * ROWS * 512),
    )(core, *arrays)


def pairs_kernel(own, apart, parts, tiles, *refs):
    core, q_in, k_in = refs[0], refs[1:1 + len(parts)], refs[1 + len(parts)]
    *outs, q, k, dq, dk, dv, row_q, col_k, bound, todo, w0, d0, w1, d1, sem = refs[2 + len(parts):]
    copies = [pltpu.make_async_copy(k_in, k, sem.at[0])]
    for ref, moves in zip(q_in, parts):
        for source, target, size in moves:
            copies.append(
                pltpu.make_async_copy(
                    ref.at[pl.ds(source, size)], q.at[pl.ds(target, size)], sem.at[len(copies)]
                )
            )
    for copy in copies:
        copy.start()
    dq[...] = jnp.zeros_like(dq)
    dk[...] = jnp.zeros_like(dk)
    dv[...] = jnp.zeros_like(dv)
    for copy in copies:
        copy.wait()
    blocks = PAIR // 256
    users_q, users_k = q[PAIR:].astype(F32), k[PAIR:].astype(F32)
    padded = jnp.concatenate([users_k, jnp.zeros((128 - SEG_ROWS, 256), F32)])
    for half in range(2):
        turned = jnp.transpose(padded[:, half * 128:half * 128 + 128])
        for r in range(blocks):
            start = r * 256 + half * 128
            col_k[start:start + 128] = jnp.broadcast_to(turned[:, r:r + 1], (128, 128))
    for r in range(blocks):
        row_q[:, r * 256:(r + 1) * 256] = users_q[r:r + 1]
    row_q[:, PAIR:] = jnp.full((1, TILE), -1.0, F32)
    for b in range(TILES):
        rows = slice(b * TILE // 256, (b + 1) * TILE // 256)
        bound[0, b] = jnp.min(users_q[rows])
        bound[1, b] = jnp.max(users_q[rows])
        bound[2, b] = jnp.min(users_k[rows])
        bound[3, b] = jnp.max(users_k[rows])

    count = jnp.int32(0)
    for kt in range(TILES):
        for qt in tiles:
            if own and qt < kt:
                continue
            some = (bound[0, qt] <= bound[3, kt]) & (bound[1, qt] >= bound[2, kt])
            todo[0, count] = qt
            todo[1, count] = kt
            todo[2, count] = qt
            count = count + some.astype(jnp.int32)
    for extra in range(3):
        todo[0, count + extra] = tiles[0]
        todo[1, count + extra] = 0
        todo[2, count + extra] = TILES
    last = (((1,), (1,)), ((), ()))
    first = (((0,), (0,)), ((), ()))

    def rows_of(tile):
        return pl.ds(pl.multiple_of(tile * TILE, TILE), TILE)

    def score(n, w_out, d_out):
        qt, kt = todo[0, n], todo[1, n]
        q_at, k_at = rows_of(qt), rows_of(kt)
        s = lax.dot_general(k[k_at, 0:128], q[q_at, 0:128], last, preferred_element_type=F32)
        p = lax.dot_general(k[k_at, 128:256], q[q_at, 128:256], last, preferred_element_type=F32)
        allowed = col_k[k_at, 0:1] == row_q[:, rows_of(todo[2, n])]
        if own:
            ahead = (qt - kt) * TILE
            allowed = allowed & (
                lax.broadcasted_iota(jnp.int32, (TILE, TILE), 1) + ahead
                >= lax.broadcasted_iota(jnp.int32, (TILE, TILE), 0)
            )
        y = jnp.where(allowed, s * HALF_SCALE, -64.0)
        t = jnp.tanh(y)
        u = 1.0 + t
        w = y * u
        d_out[...] = (p * (u + w * (1.0 - t))).astype(BF16)
        w_out[...] = w.astype(BF16)

    def gather(n, w_in, d_in):
        q_at, k_at = rows_of(todo[0, n]), rows_of(todo[1, n])
        dv[k_at, :] += jnp.dot(w_in[...], q[q_at, 128:256], preferred_element_type=F32)
        dk[k_at, :] += jnp.dot(d_in[...], q[q_at, 0:128], preferred_element_type=F32)
        dq[q_at, :] += lax.dot_general(d_in[...], k[k_at, 0:128], first, preferred_element_type=F32)

    @pl.when(count > 0)
    def _():
        score(0, w0, d0)

        def two(j, carry):
            n = 2 * j
            score(n + 1, w1, d1)
            gather(n, w0, d0)
            score(n + 2, w0, d0)
            gather(n + 1, w1, d1)
            return carry

        lax.fori_loop(0, (count + 1) // 2, two, 0)

    for out, half in zip(outs[-2:] if apart else outs[-1:], (core[0], 1 - core[0])):
        at = pl.ds(pl.multiple_of(half * ROWS, ROWS), ROWS) if apart else pl.ds(0, PAIR)
        out[:, 0:128] = (dk[at, :] * HALF_SCALE).astype(out.dtype)
        out[:, 128:256] = dv[at, :].astype(out.dtype)
    if len(tiles) == TILES:
        for out, half in zip(outs[:2], (core[0], 1 - core[0])):
            at = pl.ds(pl.multiple_of(half * ROWS, ROWS), ROWS)
            out[...] = (dq[at, :] * HALF_SCALE).astype(out.dtype)
    else:
        out, at = outs[0], slice(tiles[0] * TILE, (tiles[-1] + 1) * TILE)
        out[...] = (dq[at] * HALF_SCALE).astype(out.dtype)


WHOLE = [(0, 0, PAIR + SEG_ROWS)]
EARLY = [(0, 0, ROWS), (ROWS, PAIR, SEG_ROWS)]
USERS_ONLY = [(ROWS, PAIR, SEG_ROWS)]
LATE = [(0, ROWS, ROWS)]


def pairs(name, core, queries, parts, key, kind, tiles, area):
    anywhere = pl.BlockSpec(memory_space=pl.ANY)
    apart = name != "pairs_two"
    key_shapes = [(ROWS, 256)] * 2 if apart else [(PAIR, 256)]
    return pl.pallas_call(
        lambda *refs: pairs_kernel(name == "pairs_own", apart, parts, tiles, *refs),
        in_specs=[SMEM] + [anywhere] * (len(queries) + 1),
        out_specs=[VMEM] * (len(tiles) * TILE // ROWS + len(key_shapes)),
        out_shape=[jax.ShapeDtypeStruct((ROWS, 128), kind)] * (len(tiles) * TILE // ROWS)
        + [jax.ShapeDtypeStruct(shape, kind) for shape in key_shapes],
        scratch_shapes=[
            pltpu.VMEM((PAIR + SEG_ROWS, 256), BF16),
            pltpu.VMEM((PAIR + SEG_ROWS, 256), BF16),
            pltpu.VMEM((PAIR, 128), F32),
            pltpu.VMEM((PAIR, 128), F32),
            pltpu.VMEM((PAIR, 128), F32),
            pltpu.VMEM((1, PAIR + TILE), F32),
            pltpu.VMEM((PAIR, 128), F32),
            pltpu.SMEM((4, TILES), F32),
            pltpu.SMEM((3, TILES * TILES + 4), jnp.int32),
            pltpu.VMEM((TILE, TILE), BF16),
            pltpu.VMEM((TILE, TILE), BF16),
            pltpu.VMEM((TILE, TILE), BF16),
            pltpu.VMEM((TILE, TILE), BF16),
            pltpu.SemaphoreType.DMA((4,)),
        ],
        compiler_params=params(28),
        cost_estimate=cost(20 * area * 128, area, 8 * PAIR * 256),
    )(core, *queries, key)


def collect_kernel(place, dq, dkv, other, back_same, back_cross, far_same, far_cross, key_back,
                   gate_grad, weights,
                   left, low, high):
    core, x = place[0], place[1]
    front = core == 0
    for p in range(3):
        cols = slice(p * 128, (p + 1) * 128)
        b = other[:, cols].astype(F32)
        if p == 0:
            a = dq[...] + total(back_same[...], far_same[...])
            b = b + total(back_cross[...], far_cross[...])
        else:
            part = slice((p - 1) * 128, p * 128)
            at = pl.ds(pl.multiple_of(core * ROWS, ROWS), ROWS)
            a = dkv[:, part] + key_back[at, part].astype(F32)
        a, b = a.astype(BF16), b.astype(BF16)
        left[:, p * 256:p * 256 + 128] = jnp.where(front, a, b)
        left[:, p * 256 + 128:p * 256 + 256] = jnp.where(front, b, a)
    left[:, 768:1024] = gate_grad[...]
    far = head_block(left, weights, lax.rem(x + 2, 4)).astype(BF16)
    low[...] = far[:ROWS // 2]
    high[...] = far[ROWS // 2:]


def head_block(left, weights, dest):
    ds = pl.ds(pl.multiple_of(dest * 256, 256), 256)
    acc = None
    for p in range(4):
        term = lax.dot_general(
            left[:, p * 256:p * 256 + 256], weights[p, ds, :], (((1,), (1,)), ((), ())),
            preferred_element_type=F32,
        )
        acc = term if acc is None else acc + term
    return acc


def project_kernel(place, left, weights, after, before, own):
    x = place[1]
    after[...] = head_block(left, weights, lax.rem(x + 1, 4))
    before[...] = head_block(left, weights, lax.rem(x + 3, 4))
    own[...] = head_block(left, weights, x)


def collect(place, *arrays):
    half = jax.ShapeDtypeStruct((ROWS // 2, 256), BF16)
    return pl.pallas_call(
        collect_kernel,
        in_specs=[SMEM] + [VMEM] * 10,
        out_specs=[VMEM] * 3,
        out_shape=[jax.ShapeDtypeStruct((ROWS, 1024), BF16), half, half],
        compiler_params=params(24),
        cost_estimate=cost(2 * ROWS * 1024 * 256, 0, 8 * ROWS * 1024),
        name="collect",
    )(place, *arrays)


def project(place, left, weights):
    return pl.pallas_call(
        project_kernel,
        in_specs=[SMEM, VMEM, VMEM],
        out_specs=[VMEM] * 3,
        out_shape=[jax.ShapeDtypeStruct((ROWS, 256), F32)] * 3,
        compiler_params=params(24),
        cost_estimate=cost(2 * ROWS * 1024 * 768, 0, 8 * ROWS * 1024),
        name="project",
    )(place, left, weights)


def compute(queries, key_rows, value_rows, attn_out, gate_pre, out_grad, segments, projections):
    core = lax.axis_index("seq") % 2
    head = lax.axis_index("head")
    front = core == 0
    core_at = core.reshape(1).astype(jnp.int32)

    def in_order(kept, received):
        return jnp.where(front, kept, received), jnp.where(front, received, kept)

    def give(same, cross, target):
        same = move(same, target)
        cross = move(cross, lambda i: target(i) ^ 1)
        return same, cross

    def by_head(block):
        return in_order(block[:, :HEAD_DIM], block[:, HEAD_DIM:])

    users = (segments + 1).astype(BF16)
    users_recv = swap(users)
    kv_keep, kv_send = (
        jnp.concatenate(pair, axis=1) for pair in zip(by_head(key_rows), by_head(value_rows))
    )
    kv_recv = swap(kv_send)
    keep, send, gate_grad = by_rows(
        prepare_kernel, 3, core_at, queries, attn_out, gate_pre, out_grad
    )
    recv = swap(send)
    seg = jnp.concatenate(in_order(users, users_recv)).reshape(PAIR // 256, 256)
    seg = jnp.pad(seg, ((0, SEG_ROWS - PAIR // 256), (0, 0)))
    key = jnp.concatenate([*in_order(kv_keep, kv_recv), seg])
    key_prev = shift(key, 2)
    recv, key, seg = lax.optimization_barrier((recv, key, seg))
    low_rows, high_rows = in_order(keep, recv)
    next_a = shift(jnp.concatenate([low_rows, seg]), -2)
    next_b = shift(high_rows, -2)
    query = jnp.concatenate([low_rows, high_rows, seg])
    every, early, late = (0, 1, 2, 3), (0, 1), (2, 3)
    area = PAIR * PAIR
    dq0, dq0_other, *dkv0 = pairs(
        "pairs_own", core_at, [query], [WHOLE], key, F32, every, area // 2
    )
    next_a, dq0 = lax.optimization_barrier((next_a, dq0))
    dq1a, *dkv1a = pairs("pairs_one", core_at, [next_a], [EARLY], key, BF16, early, area // 2)
    dkv0 = [total(*terms) for terms in zip(dkv0, dkv1a)]
    query, next_a, next_b, key_prev, dq1a, dkv0 = lax.optimization_barrier(
        (query, next_a, next_b, key_prev, dq1a, dkv0)
    )
    query_far = shift(query, -6)
    dq2_same, dq2_cross, dkv2 = pairs(
        "pairs_two", core_at, [next_a, next_b], [EARLY, LATE], key_prev, BF16, every, area // 2
    )
    key_back = shift(dkv2, -2)
    next_b, dq2_same = lax.optimization_barrier((next_b, dq2_same))
    dq1b, *dkv1b = pairs(
        "pairs_one", core_at, [next_a, next_b], [USERS_ONLY, LATE], key, BF16, late, area // 2
    )
    same, cross = in_order(dq1a, dq1b)
    same, cross = total(same, dq2_same).astype(BF16), total(cross, dq2_cross).astype(BF16)
    back_same, back_cross = give(same, cross, lambda i: i + 2)
    query_far, dq1b = lax.optimization_barrier((query_far, dq1b))
    dq3_same, dq3_cross, *dkv3 = pairs(
        "pairs_three", core_at, [query_far], [WHOLE], key, BF16, every, area // 8
    )
    far_same, far_cross = give(dq3_same, dq3_cross, lambda i: i + 6)
    mine = total(dkv0[0], dkv1b[0], dkv3[0])
    back_other = jnp.where(front, key_back[ROWS:], key_back[:ROWS])
    other = total(dkv0[1], dkv1b[1], dkv3[1], back_other)
    other = jnp.concatenate([dq0_other, other], axis=1).astype(BF16)
    other = swap(other)
    place = jnp.stack([core, head]).astype(jnp.int32)
    left, low, high = collect(
        place, dq0, mine, other, back_same, back_cross, far_same, far_cross, key_back,
        gate_grad, projections,
    )

    def turn(block, by):
        return lax.ppermute(block, "head", [(i, (i + by) % 4) for i in range(4)])

    low, high = turn(low, 1), turn(high, -1)
    after, before, result = project(place, left, projections)
    half = ROWS // 2
    after = jnp.concatenate([after[:half] + low.astype(F32), after[half:]]).astype(BF16)
    before = jnp.concatenate([before[:half], before[half:] + high.astype(F32)]).astype(BF16)
    return total(result, turn(after, 1), turn(before, -1)).astype(BF16)


def solution(mesh):
    split = P("seq", "head")
    return jax.shard_map(
        compute,
        mesh=mesh,
        in_specs=(split,) * 6 + (P("seq"), P(None, None, "head")),
        out_specs=split,
        check_vma=False,
    )
```

```python
import jax
import jax.numpy as jnp
from jax import lax
from jax.experimental import pallas as pl
from jax.experimental.pallas import tpu as pltpu
from jax.sharding import PartitionSpec as P


HEAD_DIM = 128
ROWS = 1024
PAIR = 2 * ROWS
SEG_ROWS = 16
TILE = 512
TILES = PAIR // TILE
HALF_SCALE = 0.5 * HEAD_DIM ** (-0.5)
VMEM = pl.BlockSpec(memory_space=pltpu.VMEM)
SMEM = pl.BlockSpec(memory_space=pltpu.SMEM)
BF16, F32 = jnp.bfloat16, jnp.float32


def cost(flops, transcendentals, size):
    return pl.CostEstimate(flops=flops, transcendentals=transcendentals, bytes_accessed=size)


def params(mib):
    return pltpu.CompilerParams(vmem_limit_bytes=mib * 2**20)


def move(block, target):
    devices = range(lax.axis_size("seq"))
    route = [(i, target(i)) for i in devices if target(i) in devices]
    return lax.ppermute(block, "seq", route)


def shift(block, distance):
    return move(block, lambda i: i + distance)


def swap(block):
    return lax.ppermute(block, "seq", [(i, i ^ 1) for i in range(lax.axis_size("seq"))])


def total(*terms):
    return sum(t.astype(F32) for t in terms)


def silu_slope(v):
    sigma = jax.nn.sigmoid(v)
    return sigma * (1.0 + v * (1.0 - sigma))


def prepare_kernel(core, q, o, gate, grad, keep, send, gate_grad):
    for slot, out in ((0, keep), (1, send)):
        head = core[0] if slot == 0 else 1 - core[0]
        cols = pl.ds(pl.multiple_of(head * HEAD_DIM, HEAD_DIM), HEAD_DIM)
        saved = o[:, cols].astype(F32)
        centred = saved - jnp.mean(saved, axis=-1, keepdims=True)
        inverse = lax.rsqrt(jnp.mean(centred * centred, axis=-1, keepdims=True) + 1e-06)
        normed = centred * inverse
        gate_in = gate[:, cols].astype(F32)
        grad_in = grad[:, cols].astype(F32)
        gate_grad[:, cols] = (grad_in * normed * silu_slope(gate_in)).astype(BF16)
        g = grad_in * jax.nn.silu(gate_in)
        attn_grad = inverse * (
            g
            - jnp.mean(g, axis=-1, keepdims=True)
            - normed * jnp.mean(g * normed, axis=-1, keepdims=True)
        )
        out[:, 0:128] = q[:, cols]
        out[:, 128:256] = attn_grad.astype(BF16)


def by_rows(kernel, outputs, core, *arrays):
    rows = 512
    wide = pl.BlockSpec((rows, 2 * HEAD_DIM), lambda i, c: (i, 0))
    return pl.pallas_call(
        kernel,
        grid_spec=pltpu.PrefetchScalarGridSpec(
            num_scalar_prefetch=1,
            grid=(ROWS // rows,),
            in_specs=[wide] * len(arrays),
            out_specs=[wide] * outputs,
        ),
        out_shape=[jax.ShapeDtypeStruct((ROWS, 2 * HEAD_DIM), BF16)] * outputs,
        compiler_params=params(60),
        cost_estimate=cost(30 * ROWS * 256, 2 * ROWS * 256, 8 * ROWS * 512),
    )(core, *arrays)


def pairs_kernel(own, apart, bases, parts, tiles, *refs):
    core, q_in, k_in = refs[0], refs[1:1 + len(parts)], refs[1 + len(parts)]
    base = refs[2 + len(parts):2 + len(parts) + bases]
    *outs, q, k, dq, dk, dv, row_q, col_k, bound, todo, w0, d0, w1, d1, sem = refs[2 + len(parts) + bases:]
    copies = [pltpu.make_async_copy(k_in, k, sem.at[0])]
    for ref, moves in zip(q_in, parts):
        for source, target, size in moves:
            copies.append(
                pltpu.make_async_copy(
                    ref.at[pl.ds(source, size)], q.at[pl.ds(target, size)], sem.at[len(copies)]
                )
            )
    for copy in copies:
        copy.start()
    dq[...] = jnp.zeros_like(dq)
    dk[...] = jnp.zeros_like(dk)
    dv[...] = jnp.zeros_like(dv)
    for copy in copies:
        copy.wait()
    blocks = PAIR // 256
    users_q, users_k = q[PAIR:].astype(F32), k[PAIR:].astype(F32)
    padded = jnp.concatenate([users_k, jnp.zeros((128 - SEG_ROWS, 256), F32)])
    for half in range(2):
        turned = jnp.transpose(padded[:, half * 128:half * 128 + 128])
        for r in range(blocks):
            start = r * 256 + half * 128
            col_k[start:start + 128] = jnp.broadcast_to(turned[:, r:r + 1], (128, 128))
    for r in range(blocks):
        row_q[:, r * 256:(r + 1) * 256] = users_q[r:r + 1]
    row_q[:, PAIR:] = jnp.full((1, TILE), -1.0, F32)
    for b in range(TILES):
        rows = slice(b * TILE // 256, (b + 1) * TILE // 256)
        bound[0, b] = jnp.min(users_q[rows])
        bound[1, b] = jnp.max(users_q[rows])
        bound[2, b] = jnp.min(users_k[rows])
        bound[3, b] = jnp.max(users_k[rows])

    count = jnp.int32(0)
    for kt in range(TILES):
        for qt in tiles:
            if own and qt < kt:
                continue
            some = (bound[0, qt] <= bound[3, kt]) & (bound[1, qt] >= bound[2, kt])
            todo[0, count] = qt
            todo[1, count] = kt
            todo[2, count] = qt
            count = count + some.astype(jnp.int32)
    for extra in range(3):
        todo[0, count + extra] = tiles[0]
        todo[1, count + extra] = 0
        todo[2, count + extra] = TILES
    last = (((1,), (1,)), ((), ()))
    first = (((0,), (0,)), ((), ()))

    def rows_of(tile):
        return pl.ds(pl.multiple_of(tile * TILE, TILE), TILE)

    def score(n, w_out, d_out):
        qt, kt = todo[0, n], todo[1, n]
        q_at, k_at = rows_of(qt), rows_of(kt)
        s = lax.dot_general(k[k_at, 0:128], q[q_at, 0:128], last, preferred_element_type=F32)
        p = lax.dot_general(k[k_at, 128:256], q[q_at, 128:256], last, preferred_element_type=F32)
        allowed = col_k[k_at, 0:1] == row_q[:, rows_of(todo[2, n])]
        if own:
            ahead = (qt - kt) * TILE
            allowed = allowed & (
                lax.broadcasted_iota(jnp.int32, (TILE, TILE), 1) + ahead
                >= lax.broadcasted_iota(jnp.int32, (TILE, TILE), 0)
            )
        y = jnp.where(allowed, s * HALF_SCALE, -64.0)
        t = jnp.tanh(y)
        u = 1.0 + t
        w = y * u
        d_out[...] = (p * (u + w * (1.0 - t))).astype(BF16)
        w_out[...] = w.astype(BF16)

    def gather(n, w_in, d_in):
        q_at, k_at = rows_of(todo[0, n]), rows_of(todo[1, n])
        dv[k_at, :] += jnp.dot(w_in[...], q[q_at, 128:256], preferred_element_type=F32)
        dk[k_at, :] += jnp.dot(d_in[...], q[q_at, 0:128], preferred_element_type=F32)
        dq[q_at, :] += lax.dot_general(d_in[...], k[k_at, 0:128], first, preferred_element_type=F32)

    @pl.when(count > 0)
    def _():
        score(0, w0, d0)

        def two(j, carry):
            n = 2 * j
            score(n + 1, w1, d1)
            gather(n, w0, d0)
            score(n + 2, w0, d0)
            gather(n + 1, w1, d1)
            return carry

        lax.fori_loop(0, (count + 1) // 2, two, 0)

    for i, (out, half) in enumerate(zip(outs[-2:] if apart else outs[-1:], (core[0], 1 - core[0]))):
        at = pl.ds(pl.multiple_of(half * ROWS, ROWS), ROWS) if apart else pl.ds(0, PAIR)
        key_grad, value_grad = dk[at, :] * HALF_SCALE, dv[at, :]
        if bases:
            key_grad, value_grad = key_grad + base[i][:, 0:128], value_grad + base[i][:, 128:256]
        out[:, 0:128] = key_grad.astype(out.dtype)
        out[:, 128:256] = value_grad.astype(out.dtype)
    if len(tiles) == TILES:
        for out, half in zip(outs[:2], (core[0], 1 - core[0])):
            at = pl.ds(pl.multiple_of(half * ROWS, ROWS), ROWS)
            out[...] = (dq[at, :] * HALF_SCALE).astype(out.dtype)
    else:
        out, at = outs[0], slice(tiles[0] * TILE, (tiles[-1] + 1) * TILE)
        out[...] = (dq[at] * HALF_SCALE).astype(out.dtype)


WHOLE = [(0, 0, PAIR + SEG_ROWS)]
EARLY = [(0, 0, ROWS), (ROWS, PAIR, SEG_ROWS)]
USERS_ONLY = [(ROWS, PAIR, SEG_ROWS)]
LATE = [(0, ROWS, ROWS)]


def pairs(name, core, queries, parts, key, kind, tiles, area, base=()):
    anywhere = pl.BlockSpec(memory_space=pl.ANY)
    apart = name != "pairs_two"
    key_shapes = [(ROWS, 256)] * 2 if apart else [(PAIR, 256)]
    return pl.pallas_call(
        lambda *refs: pairs_kernel(name == "pairs_own", apart, len(base), parts, tiles, *refs),
        in_specs=[SMEM] + [anywhere] * (len(queries) + 1) + [VMEM] * len(base),
        out_specs=[VMEM] * (len(tiles) * TILE // ROWS + len(key_shapes)),
        out_shape=[jax.ShapeDtypeStruct((ROWS, 128), kind)] * (len(tiles) * TILE // ROWS)
        + [jax.ShapeDtypeStruct(shape, F32 if base else kind) for shape in key_shapes],
        scratch_shapes=[
            pltpu.VMEM((PAIR + SEG_ROWS, 256), BF16),
            pltpu.VMEM((PAIR + SEG_ROWS, 256), BF16),
            pltpu.VMEM((PAIR, 128), F32),
            pltpu.VMEM((PAIR, 128), F32),
            pltpu.VMEM((PAIR, 128), F32),
            pltpu.VMEM((1, PAIR + TILE), F32),
            pltpu.VMEM((PAIR, 128), F32),
            pltpu.SMEM((4, TILES), F32),
            pltpu.SMEM((3, TILES * TILES + 4), jnp.int32),
            pltpu.VMEM((TILE, TILE), BF16),
            pltpu.VMEM((TILE, TILE), BF16),
            pltpu.VMEM((TILE, TILE), BF16),
            pltpu.VMEM((TILE, TILE), BF16),
            pltpu.SemaphoreType.DMA((4,)),
        ],
        compiler_params=params(28),
        cost_estimate=cost(20 * area * 128, area, 8 * PAIR * 256),
    )(core, *queries, key, *base)


def collect_kernel(place, dq, dkv, other, back_same, back_cross, far_same, far_cross, key_back,
                   gate_grad, weights,
                   left, low, high):
    core, x = place[0], place[1]
    front = core == 0
    for p in range(3):
        cols = slice(p * 128, (p + 1) * 128)
        b = other[:, cols].astype(F32)
        if p == 0:
            a = dq[...] + total(back_same[...], far_same[...])
            b = b + total(back_cross[...], far_cross[...])
        else:
            part = slice((p - 1) * 128, p * 128)
            at = pl.ds(pl.multiple_of(core * ROWS, ROWS), ROWS)
            a = dkv[:, part] + key_back[at, part].astype(F32)
        a, b = a.astype(BF16), b.astype(BF16)
        left[:, p * 256:p * 256 + 128] = jnp.where(front, a, b)
        left[:, p * 256 + 128:p * 256 + 256] = jnp.where(front, b, a)
    left[:, 768:1024] = gate_grad[...]
    far = head_block(left, weights, lax.rem(x + 2, 4)).astype(BF16)
    low[...] = far[:ROWS // 2]
    high[...] = far[ROWS // 2:]


def head_block(left, weights, dest):
    ds = pl.ds(pl.multiple_of(dest * 256, 256), 256)
    acc = None
    for p in range(4):
        term = lax.dot_general(
            left[:, p * 256:p * 256 + 256], weights[p, ds, :], (((1,), (1,)), ((), ())),
            preferred_element_type=F32,
        )
        acc = term if acc is None else acc + term
    return acc


def project_kernel(place, left, weights, after, before, own):
    x = place[1]
    after[...] = head_block(left, weights, lax.rem(x + 1, 4))
    before[...] = head_block(left, weights, lax.rem(x + 3, 4))
    own[...] = head_block(left, weights, x)


def collect(place, *arrays):
    half = jax.ShapeDtypeStruct((ROWS // 2, 256), BF16)
    return pl.pallas_call(
        collect_kernel,
        in_specs=[SMEM] + [VMEM] * 10,
        out_specs=[VMEM] * 3,
        out_shape=[jax.ShapeDtypeStruct((ROWS, 1024), BF16), half, half],
        compiler_params=params(24),
        cost_estimate=cost(2 * ROWS * 1024 * 256, 0, 8 * ROWS * 1024),
        name="collect",
    )(place, *arrays)


def project(place, left, weights):
    return pl.pallas_call(
        project_kernel,
        in_specs=[SMEM, VMEM, VMEM],
        out_specs=[VMEM] * 3,
        out_shape=[jax.ShapeDtypeStruct((ROWS, 256), F32)] * 3,
        compiler_params=params(24),
        cost_estimate=cost(2 * ROWS * 1024 * 768, 0, 8 * ROWS * 1024),
        name="project",
    )(place, left, weights)


def compute(queries, key_rows, value_rows, attn_out, gate_pre, out_grad, segments, projections):
    core = lax.axis_index("seq") % 2
    head = lax.axis_index("head")
    front = core == 0
    core_at = core.reshape(1).astype(jnp.int32)

    def in_order(kept, received):
        return jnp.where(front, kept, received), jnp.where(front, received, kept)

    def give(same, cross, target):
        same = move(same, target)
        cross = move(cross, lambda i: target(i) ^ 1)
        return same, cross

    def by_head(block):
        return in_order(block[:, :HEAD_DIM], block[:, HEAD_DIM:])

    users = (segments + 1).astype(BF16)
    users_recv = swap(users)
    kv_keep, kv_send = (
        jnp.concatenate(pair, axis=1) for pair in zip(by_head(key_rows), by_head(value_rows))
    )
    kv_recv = swap(kv_send)
    keep, send, gate_grad = by_rows(
        prepare_kernel, 3, core_at, queries, attn_out, gate_pre, out_grad
    )
    recv = swap(send)
    seg = jnp.concatenate(in_order(users, users_recv)).reshape(PAIR // 256, 256)
    seg = jnp.pad(seg, ((0, SEG_ROWS - PAIR // 256), (0, 0)))
    key = jnp.concatenate([*in_order(kv_keep, kv_recv), seg])
    key_prev = shift(key, 2)
    recv, key, seg = lax.optimization_barrier((recv, key, seg))
    low_rows, high_rows = in_order(keep, recv)
    next_a = shift(jnp.concatenate([low_rows, seg]), -2)
    next_b = shift(high_rows, -2)
    query = jnp.concatenate([low_rows, high_rows, seg])
    every, early, late = (0, 1, 2, 3), (0, 1), (2, 3)
    area = PAIR * PAIR
    dq0, dq0_other, *dkv0 = pairs(
        "pairs_own", core_at, [query], [WHOLE], key, F32, every, area // 2
    )
    next_a, dq0 = lax.optimization_barrier((next_a, dq0))
    dq1a, *dkv0 = pairs("pairs_one", core_at, [next_a], [EARLY], key, BF16, early, area // 2, dkv0)
    query, next_a, next_b, key_prev, dq1a = lax.optimization_barrier(
        (query, next_a, next_b, key_prev, dq1a)
    )
    query_far = shift(query, -6)
    dq2_same, dq2_cross, dkv2 = pairs(
        "pairs_two", core_at, [next_a, next_b], [EARLY, LATE], key_prev, BF16, every, area // 2
    )
    key_back = shift(dkv2, -2)
    next_b, dq2_same = lax.optimization_barrier((next_b, dq2_same))
    dq1b, *dkv1b = pairs(
        "pairs_one", core_at, [next_a, next_b], [USERS_ONLY, LATE], key, BF16, late, area // 2
    )
    same, cross = in_order(dq1a, dq1b)
    same, cross = total(same, dq2_same).astype(BF16), total(cross, dq2_cross).astype(BF16)
    back_same, back_cross = give(same, cross, lambda i: i + 2)
    query_far, dq1b = lax.optimization_barrier((query_far, dq1b))
    dq3_same, dq3_cross, *dkv3 = pairs(
        "pairs_three", core_at, [query_far], [WHOLE], key, BF16, every, area // 8
    )
    far_same, far_cross = give(dq3_same, dq3_cross, lambda i: i + 6)
    mine = total(dkv0[0], dkv1b[0], dkv3[0])
    back_other = jnp.where(front, key_back[ROWS:], key_back[:ROWS])
    other = total(dkv0[1], dkv1b[1], dkv3[1], back_other)
    other = jnp.concatenate([dq0_other, other], axis=1).astype(BF16)
    other = swap(other)
    place = jnp.stack([core, head]).astype(jnp.int32)
    left, low, high = collect(
        place, dq0, mine, other, back_same, back_cross, far_same, far_cross, key_back,
        gate_grad, projections,
    )

    def turn(block, by):
        return lax.ppermute(block, "head", [(i, (i + by) % 4) for i in range(4)])

    low, high = turn(low, 1), turn(high, -1)
    after, before, result = project(place, left, projections)
    half = ROWS // 2
    after = jnp.concatenate([after[:half] + low.astype(F32), after[half:]]).astype(BF16)
    before = jnp.concatenate([before[:half], before[half:] + high.astype(F32)]).astype(BF16)
    return total(result, turn(after, 1), turn(before, -1)).astype(BF16)


def solution(mesh):
    split = P("seq", "head")
    return jax.shard_map(
        compute,
        mesh=mesh,
        in_specs=(split,) * 6 + (P("seq"), P(None, None, "head")),
        out_specs=split,
        check_vma=False,
    )
```
